32 devices in a mesh: cell: 2 (over x), ap: 8 (over z, y), sc: 2 (over core).
Axes of the slice: x: 2, y: 2, z: 4, core: 2. Of those that a mesh axis runs over, the one named last changes fastest.
Arguments:
- unsmoothed_link_guesses: bfloat16 [32, 4, 2, 128, 2048], P(('cell', 'ap'), None, None, None, 'sc'), parts along dimension 0, may hold values from -24 to 24
- received: bfloat16 [32, 4, 2, 4, 2048], P(('cell', 'ap'), None, None, None, 'sc'), parts along dimension 0, may hold values from -6 to 6
- user_power: float32 [256], P('cell'), parts along dimension 0, may hold values from 0.25 to 4
- noise_power: float32 [32], P(('cell', 'ap')), parts along dimension 0, may hold values from 0.1 to 1
- ap_gain: float32 [32, 128], P(('cell', 'ap')), parts along dimension 0, may hold values from 0.5 to 4
- user_cluster: int32 [256], P('cell'), parts along dimension 0, may hold values from 0 to 15, as said below
- serving: int32 [32, 16], P('cell'), parts along dimension 0, may hold values from 0 to 1, as said below
- cluster_owner: int32 [32, 1], P('cell'), parts along dimension 0, may hold values from 0 to 7, as said below
Outputs:
- estimates: float32 [64, 8, 4, 2, 2048], P(('cell', 'ap'), None, None, None, 'sc'), parts along dimension 0
The draws below stay inside these ranges and needn't reach their ends.
There are 2 independent parts, one for each index of `cell`. The reference program is written for one: setup_inputs(seed, part) draws one part's arguments, and reference() takes and returns one part's arrays. A program takes and returns all parts, laid end to end along the dimension named above; each array names one. Nothing has to cross between parts.
Inputs may be any that keep to these rules, and one draw needn't show every extreme that they name: `user_cluster`: each of the 16 clusters holds exactly 8 users. `serving`: column a belongs to index a // 2 of ap. Where a cluster is served by an index of ap, at least one of its access points serves it. Of the clusters that one index of ap serves, at most 2 have the same owner; in every draw some owner has exactly 2 of its clusters served by every index of ap. `cluster_owner`: at most 4 clusters have the same owner, and some owner has exactly 4.
All inputs are finite; a program needn't handle non-finite values.
Results may differ from the reference program's by a relative error of at most 0.017.
Values may be sent and summed in bfloat16 or wider, within the bound.
A program may use at most 128 MiB of HBM per device.

```python
import math
import jax
import jax.numpy as jnp
from jax import lax

AP_DEV = 2
ANTENNA_COUNT = 4
TONE_NUMBER = 2048
TAPS = 64
DATA_SYMBOLS = 4
CU = 8
OWN_MAX = 4
PEER_MAX = 2
ACCESS_POINTS = 16
CLUSTERS = 16
USER_TOTAL = 128
SLOTS = 32
N_AP = 8


def owner_and_serving(key):
    base_key = jax.random.fold_in(key, 11)
    subkeys = jax.random.split(base_key, 6)
    devices = ACCESS_POINTS // AP_DEV
    slot_count = devices * OWN_MAX
    heavy_owner = jax.random.randint(subkeys[0], (), 0, devices)
    slot_ids = jnp.arange(slot_count, dtype=jnp.int32)
    scores = jax.random.randint(subkeys[1], (slot_count,), 0, 1 << 16) * slot_count + slot_ids
    scores = jnp.where(slot_ids // OWN_MAX == heavy_owner, slot_ids - slot_count, scores)
    slot_order = jnp.argsort(scores)
    chosen = (slot_order[:CLUSTERS] // OWN_MAX).astype(jnp.int32)
    shuffled = jax.random.permutation(subkeys[2], CLUSTERS)
    owner_map = jnp.zeros((CLUSTERS,), jnp.int32).at[shuffled].set(chosen)
    cluster_ids = jnp.arange(CLUSTERS, dtype=jnp.int32)
    same_owner = owner_map[:, None] == owner_map[None, :]
    earlier = cluster_ids[None, :] < cluster_ids[:, None]
    cluster_rank = jnp.sum(same_owner & earlier, axis=1).astype(jnp.int32)
    coins = jax.random.randint(subkeys[3], (devices, CLUSTERS), 0, 2)
    before = jnp.sum(coins[:, None, :] * (same_owner & earlier).astype(jnp.int32)[None], axis=2)
    served = (coins == 1) & (before < PEER_MAX)
    device_ids = jnp.arange(devices, dtype=jnp.int32)
    turn_index = (cluster_rank[None, :] - device_ids[:, None]) % OWN_MAX
    forced = turn_index < PEER_MAX
    served = jnp.where((owner_map == heavy_owner)[None, :], forced, served)
    first_ap = jax.random.randint(subkeys[4], (devices, CLUSTERS), 0, AP_DEV)
    extra_bits = jax.random.randint(subkeys[5], (devices, CLUSTERS, AP_DEV), 0, 2)
    members = (extra_bits == 1) | (jnp.arange(AP_DEV, dtype=jnp.int32)[None, None, :] == first_ap[:, :, None])
    serving = (served[:, :, None] & members).astype(jnp.int32)
    serving = jnp.transpose(serving, (1, 0, 2)).reshape(CLUSTERS, ACCESS_POINTS)
    return (owner_map, serving)


def draw_cluster_owner(key, part):
    owner_map, serving = owner_and_serving(key)
    return owner_map[:, None].astype(jnp.int32)


def draw_serving(key, part):
    owner_map, serving = owner_and_serving(key)
    return serving.astype(jnp.int32)


def draw_user_cluster(key, part):
    shuffled = jax.random.permutation(jax.random.fold_in(key, 3), USER_TOTAL)
    return (shuffled // CU).astype(jnp.int32)


def level_of(stream_key, extent, cuts, smallest, top_value):
    gain, own = 1.0, jax.random.fold_in(stream_key, 6)
    for dim, shards_of in cuts:
        steps = jnp.exp(jax.random.uniform(jax.random.fold_in(own, dim), (shards_of,), jnp.float32, smallest / len(cuts), top_value / len(cuts)))
        gain = gain * jnp.repeat(steps, extent[dim] // shards_of).reshape([-1 if axis == dim else 1 for axis in range(len(extent))])
    return gain


def gaussian(stream_key, dims, deviation, most, shards=(), held_as=jnp.bfloat16):
    values = deviation * jax.random.normal(stream_key, dims, jnp.float32)
    if shards:
        values = values * level_of(stream_key, dims, shards, -0.22, 0.18)
    return jnp.clip(values, -most, most).astype(held_as)


def setup_inputs(seed: int = 0, part: int = 0) -> dict:
    seeds = jax.random.split(jax.random.key(seed), 9)
    part_keys = jax.random.split(jax.random.fold_in(seeds[8], part), 9)
    return {
        "unsmoothed_link_guesses": gaussian(part_keys[0], (ACCESS_POINTS, ANTENNA_COUNT, 2, USER_TOTAL, TONE_NUMBER), 4.0, 24.0, ((0, 8), (4, 2))),
        "received": gaussian(part_keys[1], (ACCESS_POINTS, ANTENNA_COUNT, 2, DATA_SYMBOLS, TONE_NUMBER), 1.0, 6.0, ((0, 8), (4, 2))),
        "user_power": jnp.clip(jnp.exp(jax.random.uniform(part_keys[2], (USER_TOTAL,), jnp.float32, math.log(0.25), math.log(4.0))), 0.25, 4.0),
        "noise_power": jnp.clip(jnp.exp(math.log(1.0) - 2.3025851 * jax.random.uniform(part_keys[3], (ACCESS_POINTS,), jnp.float32) ** level_of(part_keys[3], (ACCESS_POINTS,), ((0, 8),), -0.2, 0.2)), 0.1, 1.0),
        "ap_gain": jnp.clip(jnp.exp(math.log(4.0) - 2.0794415 * jax.random.uniform(part_keys[4], (ACCESS_POINTS, USER_TOTAL), jnp.float32) ** level_of(part_keys[4], (ACCESS_POINTS, USER_TOTAL), ((0, 8),), -0.2, 0.2)), 0.5, 4.0),
        "user_cluster": draw_user_cluster(jax.random.fold_in(jax.random.fold_in(seeds[8], part), 71), part),
        "serving": draw_serving(jax.random.fold_in(jax.random.fold_in(seeds[8], part), 71), part),
        "cluster_owner": draw_cluster_owner(jax.random.fold_in(jax.random.fold_in(seeds[8], part), 71), part),
    }


def complex_times(left_factor, right_factor):
    return (left_factor[0] * right_factor[0] - left_factor[1] * right_factor[1], left_factor[0] * right_factor[1] + left_factor[1] * right_factor[0])

def times_conj(left_factor, right_factor):
    return (left_factor[0] * right_factor[0] + left_factor[1] * right_factor[1], left_factor[1] * right_factor[0] - left_factor[0] * right_factor[1])

def hermitian_solve(cov_re, cov_im, right_re, right_im):
    dimension = cov_re.shape[0]
    factor = {}
    pivots = []
    for j in range(dimension):
        pivot_root = cov_re[j, j]
        for k in range(j):
            element = factor[j, k]
            pivot_root = pivot_root - (element[0] * element[0] + element[1] * element[1])
        pivot_root = jnp.sqrt(pivot_root)
        pivots.append(pivot_root)
        for i in range(j + 1, dimension):
            running = (cov_re[i, j], cov_im[i, j])
            for k in range(j):
                product = times_conj(factor[i, k], factor[j, k])
                running = (running[0] - product[0], running[1] - product[1])
            factor[i, j] = (running[0] / pivot_root, running[1] / pivot_root)
    forward = []
    for i in range(dimension):
        running = (right_re[i], right_im[i])
        for k in range(i):
            product = complex_times(factor[i, k], forward[k])
            running = (running[0] - product[0], running[1] - product[1])
        forward.append((running[0] / pivots[i], running[1] / pivots[i]))
    result = [None] * dimension
    for i in range(dimension - 1, -1, -1):
        running = forward[i]
        for k in range(i + 1, dimension):
            product = times_conj(result[k], factor[k, i])
            running = (running[0] - product[0], running[1] - product[1])
        result[i] = (running[0] / pivots[i], running[1] / pivots[i])
    return result

def lag_fourier_matrices(lowest_tone_hertz, tone_quantity):
    tone_hertz_values = lowest_tone_hertz + jnp.arange(tone_quantity, dtype=jnp.int32)
    lag_seconds = jnp.arange(TAPS, dtype=jnp.int32)
    rotation_angles = tone_hertz_values[:, None] * lag_seconds[None, :] % TONE_NUMBER
    angles = rotation_angles.astype(jnp.float32) * (2.0 * math.pi / TONE_NUMBER)
    return jnp.concatenate([jnp.cos(angles), jnp.sin(angles)], axis=1).astype(jnp.bfloat16)

def smoothing(h_group, lag_fourier_matrix):
    dims_shape = h_group.shape
    products = jnp.dot(h_group.reshape(-1, dims_shape[-1]), lag_fourier_matrix, preferred_element_type=jnp.float32)
    products = products.reshape(dims_shape[:-1] + (2 * TAPS,))
    coef_re = (products[:, :, 0, :, :TAPS] - products[:, :, 1, :, TAPS:]) / TONE_NUMBER
    coef_im = (products[:, :, 0, :, TAPS:] + products[:, :, 1, :, :TAPS]) / TONE_NUMBER
    return jnp.stack([coef_re, coef_im], axis=2)

def rebuild(coefficients, lag_fourier_matrix):
    coef_b = coefficients.astype(jnp.bfloat16)
    real_rows = jnp.concatenate([coef_b[:, :, 0], coef_b[:, :, 1]], axis=-1)
    imag_rows = jnp.concatenate([coef_b[:, :, 1], -coef_b[:, :, 0]], axis=-1)
    stacked = jnp.stack([real_rows, imag_rows], axis=2)
    dims_shape = stacked.shape
    smooth = jnp.dot(stacked.reshape(-1, 2 * TAPS), lag_fourier_matrix.T, preferred_element_type=jnp.float32)
    return smooth.reshape(dims_shape[:-1] + (lag_fourier_matrix.shape[0],))

def local_estimates(smooth, power_row, noise_level, right_side, weight_row):
    antennas = smooth.shape[0]
    scaled = smooth * (power_row / smooth.shape[2])[None, None, :, None]
    gram_sums = jnp.einsum('icuf,jduf->icjdf', scaled, smooth, precision=lax.Precision.HIGHEST)
    cov_re = gram_sums[:, 0, :, 0] + gram_sums[:, 1, :, 1] + noise_level * jnp.eye(antennas, dtype=smooth.dtype)[:, :, None]
    cov_im = gram_sums[:, 1, :, 0] - gram_sums[:, 0, :, 1]
    signal = right_side.astype(jnp.float32)
    solved = hermitian_solve(cov_re, cov_im, signal[:, 0], signal[:, 1])
    est_re = smooth[0, 0][:, None, :] * solved[0][0][None] + smooth[0, 1][:, None, :] * solved[0][1][None]
    est_im = smooth[0, 0][:, None, :] * solved[0][1][None] - smooth[0, 1][:, None, :] * solved[0][0][None]
    for i in range(1, antennas):
        est_re = est_re + smooth[i, 0][:, None, :] * solved[i][0][None] + smooth[i, 1][:, None, :] * solved[i][1][None]
        est_im = est_im + smooth[i, 0][:, None, :] * solved[i][1][None] - smooth[i, 1][:, None, :] * solved[i][0][None]
    return weight_row[:, None, None, None] * jnp.stack([est_re, est_im], axis=2)

def reference(unsmoothed_link_guesses, received, user_power, noise_power, ap_gain, user_cluster, serving, cluster_owner):
    lag_fourier_matrix = lag_fourier_matrices(0, TONE_NUMBER)
    cluster_ids = jnp.arange(CLUSTERS, dtype=jnp.int32)
    onehot = (user_cluster[:, None] == cluster_ids[None, :]).astype(jnp.float32)
    serve_user = jnp.dot(onehot, serving.astype(jnp.float32), precision=lax.Precision.HIGHEST)
    weights = serve_user.T * ap_gain
    totals = lax.optimization_barrier(jnp.sum(weights, axis=0))

    def group_step(carry, inputs):
        h_group, right_group, noise_group, weight_group = inputs
        smooth = rebuild(smoothing(h_group, lag_fourier_matrix), lag_fourier_matrix)
        partial_value = local_estimates(smooth[0], user_power, noise_group[0], right_group[0], weight_group[0])
        for station in range(1, AP_DEV):
            partial_value = partial_value + local_estimates(smooth[station], user_power, noise_group[station], right_group[station], weight_group[station])
        rounded = lax.optimization_barrier(partial_value.astype(jnp.bfloat16))
        return (carry + rounded.astype(jnp.float32), None)
    inputs = (unsmoothed_link_guesses.reshape((N_AP, AP_DEV) + unsmoothed_link_guesses.shape[1:]), received.reshape((N_AP, AP_DEV) + received.shape[1:]), noise_power.reshape(N_AP, AP_DEV), weights.reshape(N_AP, AP_DEV, USER_TOTAL))
    initial = jnp.zeros((USER_TOTAL, DATA_SYMBOLS, 2, TONE_NUMBER), jnp.float32)
    numerator, _ = lax.scan(group_step, initial, inputs)
    decoded = numerator / (1.0 + totals)[:, None, None, None]
    owner_map = cluster_owner[:, 0]
    cluster_rank = lax.optimization_barrier(jnp.sum((owner_map[:, None] == owner_map[None, :]) & (cluster_ids[None, :] < cluster_ids[:, None]), axis=1)).astype(jnp.int32)
    user_ids = jnp.arange(USER_TOTAL, dtype=jnp.int32)
    position = lax.optimization_barrier(jnp.sum((user_cluster[:, None] == user_cluster[None, :]) & (user_ids[None, :] < user_ids[:, None]), axis=1)).astype(jnp.int32)
    slot_index = (owner_map[user_cluster] * OWN_MAX + cluster_rank[user_cluster]).astype(jnp.int32)
    estimates = jnp.zeros((SLOTS, CU, DATA_SYMBOLS, 2, TONE_NUMBER), jnp.float32).at[slot_index, position].set(decoded)
    return estimates
```

```python
import functools
import math

import jax
import jax.numpy as jnp
import numpy as np
from jax import lax
from jax.experimental import pallas as pl
from jax.experimental.pallas import tpu as pltpu
from jax.sharding import PartitionSpec as P

TONE_NUMBER = 2048
TAPS = 64
CU = 8
OWN_MAX = 4
PEER_MAX = 2
MESH = pl.DeviceIdType.MESH
LANES = 128


def complex_times(left_factor, right_factor):
    return (
        left_factor[0] * right_factor[0] - left_factor[1] * right_factor[1],
        left_factor[0] * right_factor[1] + left_factor[1] * right_factor[0],
    )


def times_conj(left_factor, right_factor):
    return (
        left_factor[0] * right_factor[0] + left_factor[1] * right_factor[1],
        left_factor[1] * right_factor[0] - left_factor[0] * right_factor[1],
    )


def hermitian_solve(cov_re, cov_im, right):
    dimension = len(cov_re)
    factor = {}
    inverses = []
    for j in range(dimension):
        pivot = cov_re[j][j]
        for k in range(j):
            element = factor[j, k]
            pivot = pivot - (element[0] * element[0] + element[1] * element[1])
        inverse = 1.0 / jnp.sqrt(pivot)
        inverses.append(inverse)
        for i in range(j + 1, dimension):
            running = (cov_re[i][j], cov_im[i][j])
            for k in range(j):
                product = times_conj(factor[i, k], factor[j, k])
                running = (running[0] - product[0], running[1] - product[1])
            factor[i, j] = (running[0] * inverse, running[1] * inverse)
    forward = []
    for i in range(dimension):
        running = right[i]
        for k in range(i):
            product = complex_times(factor[i, k], forward[k])
            running = (running[0] - product[0], running[1] - product[1])
        forward.append((running[0] * inverses[i], running[1] * inverses[i]))
    result = [None] * dimension
    for i in range(dimension - 1, -1, -1):
        running = forward[i]
        for k in range(i + 1, dimension):
            product = times_conj(result[k], factor[k, i])
            running = (running[0] - product[0], running[1] - product[1])
        result[i] = (running[0] * inverses[i], running[1] * inverses[i])
    return result


def delay_tables(parts, tones):
    made = []
    for part in range(parts):
        values = part * tones + np.arange(tones, dtype=np.int32)
        rotation = np.arange(TAPS, dtype=np.int32)[:, None] * values[None, :] % TONE_NUMBER
        angles = rotation.astype(np.float32) * np.float32(2.0 * math.pi / TONE_NUMBER)
        cosine, sine = np.cos(angles), np.sin(angles)
        made.append(
            np.concatenate(
                [
                    np.concatenate([cosine, sine], axis=0),
                    np.concatenate([-sine, cosine], axis=0),
                ],
                axis=1,
            )
        )
    return np.stack(made).astype(jnp.bfloat16)


def exact_dot(left, right, dims):
    return lax.dot_general(
        left.astype(jnp.bfloat16),
        right.astype(jnp.bfloat16),
        (dims, ((), ())),
        preferred_element_type=jnp.float32,
    )


def iota(shape, dim):
    return lax.broadcasted_iota(jnp.int32, shape, dim).astype(jnp.float32)


def user_tables(user_cluster, serving, owner, clusters, users, group, n):
    onehot = (iota((clusters, users), 0) == user_cluster.astype(jnp.float32)).astype(jnp.float32)
    owner_col = owner.astype(jnp.float32)
    square = (clusters, clusters)
    rows, cols = iota(square, 0), iota(square, 1)
    owner_row = jnp.sum(jnp.where(rows == cols, owner_col, 0.0), axis=0, keepdims=True)
    same = owner_col == owner_row
    earlier = jnp.where(same & (cols < rows), 1.0, 0.0)
    serve = serving.astype(jnp.float32)
    pair = jnp.where(
        jnp.floor((iota((group * n, n), 0) + 0.5) * (1.0 / group)) == iota((group * n, n), 1),
        1.0,
        0.0,
    )
    served = jnp.where(exact_dot(serve, pair, ((1,), (0,))) > 0.5, 1.0, 0.0)
    before = exact_dot(earlier, served, ((1,), (0,)))
    rank = jnp.sum(earlier, axis=1, keepdims=True)
    owner_u = jnp.sum(onehot * owner_col, axis=0, keepdims=True)
    rank_u = jnp.sum(onehot * rank, axis=0, keepdims=True)
    served_u = exact_dot(served, onehot, ((0,), (0,)))
    before_u = exact_dot(before, onehot, ((0,), (0,)))
    serve_u = exact_dot(serve, onehot, ((0,), (0,)))
    equal = exact_dot(onehot, onehot, ((0,), (0,)))
    both = (users, users)
    position = jnp.sum(
        jnp.where(iota(both, 0) < iota(both, 1), equal, 0.0), axis=0, keepdims=True
    )
    return owner_u, rank_u, served_u, before_u, serve_u, position


def first_kernel(
    n,
    chunks,
    ring_of,
    guess_hbm,
    received_ref,
    power_ref,
    noise_ref,
    gain_ref,
    cluster_ref,
    serving_ref,
    owner_ref,
    table_hbm,
    coef_all,
    solved_all,
    wrow_ref,
    rank_ref,
    guess,
    table,
    half,
    other,
    coef_send,
    coef_b,
    gains,
    pick,
    power_wide,
    smooth,
    cov,
    own,
    guess_sem,
    table_sem,
    half_send_sem,
    half_recv_sem,
    gain_send_sem,
    gain_recv_sem,
    coef_send_sem,
    coef_recv_sem,
    ring_send_sem,
    ring_recv_sem,
    local_sem,
):
    stations, antennas, _, users, tones = guess.shape
    pieces = stations * antennas
    block = PEER_MAX * CU
    clusters = serving_ref.shape[0]
    me = lax.axis_index("ap")
    part = lax.axis_index("sc")
    node, place = ring_of
    spot = place(me)
    right = node(lax.rem(spot + 1, n))
    left = node(lax.rem(spot + n - 1, n))

    table_copy = pltpu.make_async_copy(table_hbm.at[part], table, table_sem)
    table_copy.start()
    guess_copies = []
    for q in range(pieces):
        a, i = q // antennas, q % antennas
        copy = pltpu.make_async_copy(guess_hbm.at[a, i], guess.at[a, i], guess_sem.at[q])
        copy.start()
        guess_copies.append(copy)

    barrier = pltpu.get_barrier_semaphore()
    pl.semaphore_signal(barrier, inc=1, device_id={"sc": 1 - part}, device_id_type=MESH)
    for k in range(1, n):
        pl.semaphore_signal(
            barrier, inc=1, device_id={"ap": lax.rem(me + k, n)}, device_id_type=MESH
        )

    owner_u, rank_u, served_u, before_u, serve_u, position = user_tables(
        cluster_ref[...], serving_ref[...], owner_ref[...], clusters, users, stations, n
    )
    mef = me.astype(jnp.float32)
    mine = iota((n, users), 0) == mef
    served_me = jnp.sum(jnp.where(mine, served_u, 0.0), axis=0, keepdims=True)
    before_me = jnp.sum(jnp.where(mine, before_u, 0.0), axis=0, keepdims=True)
    target = jnp.where(
        served_me > 0.5, owner_u * block + before_me * CU + position, -1.0
    )
    pick[...] = jnp.where(iota((n * block, users), 0) == target, 1.0, 0.0).astype(jnp.bfloat16)
    wide = jnp.broadcast_to(power_ref[...] * (1.0 / users), (LANES, users))
    power_wide[...] = jnp.transpose(wide)

    pl.semaphore_wait(barrier, n)

    gain_copies = []
    for k in range(1, n):
        peer = lax.rem(me + k, n)
        copy = pltpu.make_async_remote_copy(
            src_ref=gain_ref,
            dst_ref=gains.at[me],
            send_sem=gain_send_sem.at[k],
            recv_sem=gain_recv_sem.at[n - k],
            device_id={"ap": peer},
            device_id_type=MESH,
        )
        copy.start()
        gain_copies.append(copy)
    gains[me] = gain_ref[...]

    table_copy.wait()
    half_copies = []
    contract = (((1,), (1,)), ((), ()))
    for q in range(pieces):
        a, i = q // antennas, q % antennas
        guess_copies[q].wait()
        sums = lax.dot_general(
            guess[a, i, 0], table[:, :tones], contract, preferred_element_type=jnp.float32
        ) + lax.dot_general(
            guess[a, i, 1], table[:, tones:], contract, preferred_element_type=jnp.float32
        )
        half[q] = (sums * (1.0 / TONE_NUMBER)).astype(jnp.bfloat16)
        copy = pltpu.make_async_remote_copy(
            src_ref=half.at[q],
            dst_ref=other.at[q],
            send_sem=half_send_sem.at[q],
            recv_sem=half_recv_sem.at[q],
            device_id={"sc": 1 - part},
            device_id_type=MESH,
        )
        copy.start()
        half_copies.append(copy)
    for q in range(pieces):
        half_copies[q].wait_recv()
        total = (half[q].astype(jnp.float32) + other[q].astype(jnp.float32)).astype(jnp.bfloat16)
        coef_b[pl.ds(q * users, users), :] = total
        chosen = jnp.dot(pick[...], total, preferred_element_type=jnp.float32)
        coef_send[:, q] = chosen.astype(jnp.bfloat16).reshape(n, block, 2 * TAPS)
    coef_copies = []
    for k in range(1, n):
        peer = lax.rem(me + k, n)
        copy = pltpu.make_async_remote_copy(
            src_ref=coef_send.at[peer],
            dst_ref=coef_all.at[me],
            send_sem=coef_send_sem.at[k],
            recv_sem=coef_recv_sem.at[n - k],
            device_id={"ap": peer},
            device_id_type=MESH,
        )
        copy.start()
        coef_copies.append(copy)
    own_coef = pltpu.make_async_copy(coef_send.at[me], coef_all.at[me], local_sem.at[chunks])
    own_coef.start()

    width = tones // chunks
    symbols = received_ref.shape[3]
    rows = stations * symbols
    ring_copies = {}
    reach = {}
    for c in range(chunks):
        far, near = n // 2, n - 1 - n // 2
        reach[c] = (far, near) if c % 2 == 0 else (near, far)

    def ring_start(c, direction, step):
        if step >= reach[c][direction]:
            return
        if step > 0:
            ring_copies[c, direction, step - 1].wait_recv()
        back = lax.rem(spot + n - step, n) if direction == 0 else lax.rem(spot + step, n)
        origin = node(back)
        source = own.at[c] if step == 0 else solved_all.at[origin, c]
        copy = pltpu.make_async_remote_copy(
            src_ref=source,
            dst_ref=solved_all.at[origin, c],
            send_sem=ring_send_sem.at[direction, c, step],
            recv_sem=ring_recv_sem.at[direction, c, step],
            device_id={"ap": right if direction == 0 else left},
            device_id_type=MESH,
        )
        copy.start()
        ring_copies[c, direction, step] = copy

    local_copies = []
    steps = max(max(r) for r in reach.values())
    entries = [(i, j) for i in range(antennas) for j in range(i + 1)]
    top = lax.broadcasted_iota(jnp.int32, (rows, 1), 0) < symbols
    noise = jnp.full((rows, 1), noise_ref[stations - 1], jnp.float32)
    for a in range(stations - 1):
        noise = jnp.where(
            (lax.broadcasted_iota(jnp.int32, (rows, 1), 0) // symbols) == a, noise_ref[a], noise
        )
    for c in range(chunks):
        base = c * width
        for reim in range(2):
            columns = table[:, reim * tones + base : reim * tones + base + width]
            smooth[reim] = jnp.dot(coef_b[...], columns, preferred_element_type=jnp.float32)
        for a in range(stations):
            for l in range(width // LANES):
                lanes = pl.ds(l * LANES, LANES)

                def body(step, sums, a=a, lanes=lanes):
                    sums = list(sums)
                    for w in range(2):
                        row = (step * 2 + w) * 8
                        scale = power_wide[pl.ds(pl.multiple_of(row, 8), 8), :]
                        re, im = [], []
                        for i in range(antennas):
                            at = pl.multiple_of((a * antennas + i) * users + row, 8)
                            re.append(smooth[0, pl.ds(at, 8), lanes])
                            im.append(smooth[1, pl.ds(at, 8), lanes])
                        at = 0
                        for i in range(antennas):
                            sre, sim = re[i] * scale, im[i] * scale
                            for j in range(i + 1):
                                sums[at] = sums[at] + (sre * re[j] + sim * im[j])
                                at += 1
                                if j < i:
                                    sums[at] = sums[at] + (sim * re[j] - sre * im[j])
                                    at += 1
                    return tuple(sums)

                zero = jnp.zeros((8, LANES), jnp.float32)
                sums = lax.fori_loop(0, users // 16, body, (zero,) * (antennas * antennas))
                for e in range(antennas * antennas):
                    value = jnp.sum(sums[e], axis=0, keepdims=True)
                    cov[e, a * symbols : (a + 1) * symbols, lanes] = jnp.broadcast_to(
                        value, (symbols, LANES)
                    )
        cov_re = [[None] * antennas for _ in range(antennas)]
        cov_im = [[None] * antennas for _ in range(antennas)]
        at = 0
        for i, j in entries:
            cov_re[i][j] = cov[at]
            at += 1
            if i == j:
                cov_re[i][j] = cov_re[i][j] + noise
            else:
                cov_im[i][j] = cov[at]
                at += 1
        signal = []
        for i in range(antennas):
            signal.append(
                tuple(
                    jnp.concatenate(
                        [
                            received_ref[a, i, reim, :, base : base + width].astype(jnp.float32)
                            for a in range(stations)
                        ],
                        axis=0,
                    )
                    for reim in range(2)
                )
            )
        solved = hermitian_solve(cov_re, cov_im, signal)
        for i in range(antennas):
            joined = jnp.concatenate([solved[i][0], solved[i][1]], axis=0)
            own[c, pl.ds(i * 2 * rows, 2 * rows), :] = joined.astype(jnp.bfloat16)
        copy = pltpu.make_async_copy(own.at[c], solved_all.at[me, c], local_sem.at[c])
        copy.start()
        local_copies.append(copy)
        for d in range(c + 1):
            for direction in range(2):
                ring_start(d, direction, c - d)
    for late in range(chunks, chunks + steps):
        for d in range(chunks):
            for direction in range(2):
                if late - d > 0:
                    ring_start(d, direction, late - d)

    for copy in gain_copies:
        copy.wait_recv()
    weights = []
    totals = jnp.zeros((1, users), jnp.float32)
    for p in range(n):
        for a in range(stations):
            row = serve_u[p * stations + a : p * stations + a + 1] * gains[p, a : a + 1, :]
            weights.append(row)
            totals = totals + row
    scale = 1.0 / (1.0 + totals)
    for p in range(n):
        goal = jnp.where(
            (owner_u == mef) & (served_u[p : p + 1] > 0.5),
            before_u[p : p + 1] * CU + position,
            -1.0,
        )
        hits = iota((block, users), 0) == goal
        for a in range(stations):
            value = jnp.sum(
                jnp.where(hits, weights[p * stations + a] * scale, 0.0), axis=1, keepdims=True
            )
            wrow_ref[p, a] = jnp.broadcast_to(value, (block, LANES))
        for k in range(PEER_MAX):
            value = jnp.sum(
                jnp.where(hits[k * CU : k * CU + 1], rank_u, 0.0), axis=1, keepdims=True
            )
            rank_ref[p * PEER_MAX + k : p * PEER_MAX + k + 1, :] = jnp.broadcast_to(
                value, (1, LANES)
            ).astype(jnp.int32)

    for copy in half_copies:
        copy.wait_send()
    for copy in gain_copies:
        copy.wait_send()
    for copy in coef_copies:
        copy.wait()
    own_coef.wait()
    for copy in local_copies:
        copy.wait()
    for (c, direction, step), copy in ring_copies.items():
        if step == reach[c][direction] - 1:
            copy.wait_recv()
        copy.wait_send()


def second_kernel(
    n, stations, antennas, rank_ref, coef_ref, wrow_ref, solved_ref, table_hbm, out_ref,
    table, solved, smooth, table_sem,
):
    width = solved_ref.shape[-1]
    tones = table.shape[-1] // 2
    block = PEER_MAX * CU
    symbols = out_ref.shape[1]
    rows = stations * symbols
    pieces = stations * antennas
    g = pl.program_id(0)

    @pl.when(g == 0)
    def _():
        copy = pltpu.make_async_copy(table_hbm.at[lax.axis_index("sc")], table, table_sem)
        copy.start()
        copy.wait()

    out_ref[...] = jnp.zeros_like(out_ref)

    def peer(p, carry):
        solved[...] = solved_ref[p, 0].astype(jnp.float32)
        coefs = coef_ref[p].reshape(pieces * block, 2 * TAPS)
        for reim in range(2):
            columns = table[:, pl.ds(pl.multiple_of(reim * tones + g * width, LANES), width)]
            smooth[reim] = jnp.dot(coefs, columns, preferred_element_type=jnp.float32)
        for l in range(width // LANES):
            lanes = pl.ds(l * LANES, LANES)
            sums = [[[None, None] for _ in range(symbols)] for _ in range(PEER_MAX)]
            for a in range(stations):
                weight = [wrow_ref[p, a, pl.ds(k * CU, CU), :] for k in range(PEER_MAX)]
                for i in range(antennas):
                    re, im = [], []
                    for k in range(PEER_MAX):
                        at = (a * antennas + i) * block + k * CU
                        re.append(smooth[0, pl.ds(at, CU), lanes] * weight[k])
                        im.append(smooth[1, pl.ds(at, CU), lanes] * weight[k])
                    for s in range(symbols):
                        first = i * 2 * rows + a * symbols + s
                        sre = solved[pl.ds(first, 1), lanes]
                        sim = solved[pl.ds(first + rows, 1), lanes]
                        for k in range(PEER_MAX):
                            new_re = re[k] * sre + im[k] * sim
                            new_im = re[k] * sim - im[k] * sre
                            old = sums[k][s]
                            if old[0] is not None:
                                new_re, new_im = old[0] + new_re, old[1] + new_im
                            sums[k][s] = [new_re, new_im]
            for k in range(PEER_MAX):
                slot = rank_ref[p * PEER_MAX + k, 0]
                for s in range(symbols):
                    for reim in range(2):
                        out_ref[slot, s, reim, :, lanes] += sums[k][s][reim]
        return carry

    lax.fori_loop(0, n, peer, 0)


def ring_functions(mesh):
    n = mesh.shape["ap"]
    half = n // 2

    def plain(q):
        return q

    def node(q):
        upper = q // half
        return (1 - upper) * 2 * q + upper * (2 * (n - q) - 1)

    def place(d):
        odd = d % 2
        return (1 - odd) * (d // 2) + odd * (n - (d + 1) // 2)

    if n % 2:
        return plain, plain
    try:
        axes = list(mesh.axis_names)
        line = np.moveaxis(mesh.devices, axes.index("ap"), 0).reshape(n, -1)[:, 0]
        spots = [tuple(d.coords) for d in line]
        sizes = [max(s[x] for s in spots) + 1 for x in range(3)]

        def length(order):
            far = 0
            for q in range(n):
                one, two = spots[order(q)], spots[order((q + 1) % n)]
                far += sum(
                    min(abs(one[x] - two[x]), sizes[x] - abs(one[x] - two[x])) for x in range(3)
                )
            return far

        if length(plain) < length(node):
            return plain, plain
    except (AttributeError, TypeError):
        pass
    return node, place


def local(
    n,
    parts,
    ring_of,
    unsmoothed_link_guesses,
    received,
    user_power,
    noise_power,
    ap_gain,
    user_cluster,
    serving,
    cluster_owner,
):
    stations, antennas, _, users, tones = unsmoothed_link_guesses.shape
    symbols = received.shape[3]
    pieces = stations * antennas
    block = PEER_MAX * CU
    rows = stations * symbols
    chunks = 4
    width = tones // chunks
    steps = n // 2
    table = jnp.asarray(delay_tables(parts, tones))
    vmem = pl.BlockSpec(memory_space=pltpu.VMEM)
    smem = pl.BlockSpec(memory_space=pltpu.SMEM)
    anywhere = pl.BlockSpec(memory_space=pl.ANY)
    dma = pltpu.SemaphoreType.DMA
    bf16, f32 = jnp.bfloat16, jnp.float32
    coef_all, solved_all, wrow, rank = pl.pallas_call(
        functools.partial(first_kernel, n, chunks, ring_of),
        out_shape=(
            jax.ShapeDtypeStruct((n, pieces, block, 2 * TAPS), bf16),
            jax.ShapeDtypeStruct((n, chunks, antennas * 2 * rows, width), bf16),
            jax.ShapeDtypeStruct((n, stations, block, LANES), f32),
            jax.ShapeDtypeStruct((n * PEER_MAX, LANES), jnp.int32),
        ),
        in_specs=[anywhere, vmem, vmem, smem, vmem, vmem, vmem, vmem, anywhere],
        out_specs=(anywhere, anywhere, vmem, vmem),
        scratch_shapes=[
            pltpu.VMEM((stations, antennas, 2, users, tones), bf16),
            pltpu.VMEM((2 * TAPS, 2 * tones), bf16),
            pltpu.VMEM((pieces, users, 2 * TAPS), bf16),
            pltpu.VMEM((pieces, users, 2 * TAPS), bf16),
            pltpu.VMEM((n, pieces, block, 2 * TAPS), bf16),
            pltpu.VMEM((pieces * users, 2 * TAPS), bf16),
            pltpu.VMEM((n, stations, users), f32),
            pltpu.VMEM((n * block, users), bf16),
            pltpu.VMEM((users, LANES), f32),
            pltpu.VMEM((2, pieces * users, width), f32),
            pltpu.VMEM((antennas * antennas, rows, width), f32),
            pltpu.VMEM((chunks, antennas * 2 * rows, width), bf16),
            dma((pieces,)),
            dma,
            dma((pieces,)),
            dma((pieces,)),
            dma((n,)),
            dma((n,)),
            dma((n,)),
            dma((n,)),
            dma((2, chunks, steps)),
            dma((2, chunks, steps)),
            dma((chunks + 1,)),
        ],
        compiler_params=pltpu.CompilerParams(
            collective_id=0, has_side_effects=True, vmem_limit_bytes=48 * 1024 * 1024
        ),
        name="smooth_and_solve",
    )(
        unsmoothed_link_guesses,
        received,
        user_power.reshape(1, users),
        noise_power,
        ap_gain,
        user_cluster.reshape(1, users),
        serving,
        cluster_owner,
        table,
    )
    combined = pl.pallas_call(
        functools.partial(second_kernel, n, stations, antennas),
        grid=(chunks,),
        out_shape=jax.ShapeDtypeStruct((OWN_MAX, symbols, 2, CU, tones), f32),
        in_specs=[
            smem,
            pl.BlockSpec((n, pieces, block, 2 * TAPS), lambda g: (0, 0, 0, 0)),
            pl.BlockSpec((n, stations, block, LANES), lambda g: (0, 0, 0, 0)),
            pl.BlockSpec((n, 1, antennas * 2 * rows, width), lambda g: (0, g, 0, 0)),
            anywhere,
        ],
        out_specs=pl.BlockSpec((OWN_MAX, symbols, 2, CU, width), lambda g: (0, 0, 0, 0, g)),
        scratch_shapes=[
            pltpu.VMEM((2 * TAPS, 2 * tones), bf16),
            pltpu.VMEM((antennas * 2 * rows, width), f32),
            pltpu.VMEM((2, pieces * block, width), f32),
            dma,
        ],
        name="combine",
    )(rank, coef_all, wrow, solved_all, table)
    return jnp.transpose(combined, (0, 3, 1, 2, 4))


def solution(mesh):
    placed = (
        P(("cell", "ap"), None, None, None, "sc"),
        P(("cell", "ap"), None, None, None, "sc"),
        P("cell"),
        P(("cell", "ap")),
        P(("cell", "ap"), None),
        P("cell"),
        P("cell", None),
        P("cell", None),
    )
    return jax.shard_map(
        functools.partial(local, mesh.shape["ap"], mesh.shape["sc"], ring_functions(mesh)),
        mesh=mesh,
        in_specs=placed,
        out_specs=P(("cell", "ap"), None, None, None, "sc"),
        check_vma=False,
    )
```

```python
import functools
import math

import jax
import jax.numpy as jnp
import numpy as np
from jax import lax
from jax.experimental import pallas as pl
from jax.experimental.pallas import tpu as pltpu
from jax.sharding import PartitionSpec as P

TONE_NUMBER = 2048
TAPS = 64
CU = 8
OWN_MAX = 4
PEER_MAX = 2
MESH = pl.DeviceIdType.MESH
LANES = 128


def complex_times(left_factor, right_factor):
    return (
        left_factor[0] * right_factor[0] - left_factor[1] * right_factor[1],
        left_factor[0] * right_factor[1] + left_factor[1] * right_factor[0],
    )


def times_conj(left_factor, right_factor):
    return (
        left_factor[0] * right_factor[0] + left_factor[1] * right_factor[1],
        left_factor[1] * right_factor[0] - left_factor[0] * right_factor[1],
    )


def hermitian_solve(cov_re, cov_im, right):
    dimension = len(cov_re)
    factor = {}
    inverses = []
    for j in range(dimension):
        pivot = cov_re[j][j]
        for k in range(j):
            element = factor[j, k]
            pivot = pivot - (element[0] * element[0] + element[1] * element[1])
        inverse = 1.0 / jnp.sqrt(pivot)
        inverses.append(inverse)
        for i in range(j + 1, dimension):
            running = (cov_re[i][j], cov_im[i][j])
            for k in range(j):
                product = times_conj(factor[i, k], factor[j, k])
                running = (running[0] - product[0], running[1] - product[1])
            factor[i, j] = (running[0] * inverse, running[1] * inverse)
    forward = []
    for i in range(dimension):
        running = right[i]
        for k in range(i):
            product = complex_times(factor[i, k], forward[k])
            running = (running[0] - product[0], running[1] - product[1])
        forward.append((running[0] * inverses[i], running[1] * inverses[i]))
    result = [None] * dimension
    for i in range(dimension - 1, -1, -1):
        running = forward[i]
        for k in range(i + 1, dimension):
            product = times_conj(result[k], factor[k, i])
            running = (running[0] - product[0], running[1] - product[1])
        result[i] = (running[0] * inverses[i], running[1] * inverses[i])
    return result


def delay_tables(parts, tones):
    made = []
    for part in range(parts):
        values = part * tones + np.arange(tones, dtype=np.int32)
        rotation = np.arange(TAPS, dtype=np.int32)[:, None] * values[None, :] % TONE_NUMBER
        angles = rotation.astype(np.float32) * np.float32(2.0 * math.pi / TONE_NUMBER)
        cosine, sine = np.cos(angles), np.sin(angles)
        made.append(
            np.concatenate(
                [
                    np.concatenate([cosine, sine], axis=0),
                    np.concatenate([-sine, cosine], axis=0),
                ],
                axis=1,
            )
        )
    return np.stack(made).astype(jnp.bfloat16)


def exact_dot(left, right, dims):
    return lax.dot_general(
        left.astype(jnp.bfloat16),
        right.astype(jnp.bfloat16),
        (dims, ((), ())),
        preferred_element_type=jnp.float32,
    )


def iota(shape, dim):
    return lax.broadcasted_iota(jnp.int32, shape, dim).astype(jnp.float32)


def user_tables(user_cluster, serving, owner, clusters, users, group, n):
    onehot = (iota((clusters, users), 0) == user_cluster.astype(jnp.float32)).astype(jnp.float32)
    owner_row = owner.astype(jnp.float32)
    square = (clusters, clusters)
    rows, cols = iota(square, 0), iota(square, 1)
    owner_col = jnp.sum(jnp.where(rows == cols, owner_row, 0.0), axis=1, keepdims=True)
    same = owner_col == owner_row
    earlier = jnp.where(same & (cols < rows), 1.0, 0.0)
    serve = serving.astype(jnp.float32)
    pair = jnp.where(
        jnp.floor((iota((group * n, n), 0) + 0.5) * (1.0 / group)) == iota((group * n, n), 1),
        1.0,
        0.0,
    )
    served = jnp.where(exact_dot(serve, pair, ((1,), (0,))) > 0.5, 1.0, 0.0)
    before = exact_dot(earlier, served, ((1,), (0,)))
    rank = jnp.sum(earlier, axis=1, keepdims=True)
    owner_u = jnp.sum(onehot * owner_col, axis=0, keepdims=True)
    rank_u = jnp.sum(onehot * rank, axis=0, keepdims=True)
    served_u = exact_dot(served, onehot, ((0,), (0,)))
    before_u = exact_dot(before, onehot, ((0,), (0,)))
    serve_u = exact_dot(serve, onehot, ((0,), (0,)))
    equal = exact_dot(onehot, onehot, ((0,), (0,)))
    both = (users, users)
    position = jnp.sum(
        jnp.where(iota(both, 0) < iota(both, 1), equal, 0.0), axis=0, keepdims=True
    )
    return owner_u, rank_u, served_u, before_u, serve_u, position


def first_kernel(
    n,
    chunks,
    ring_of,
    guess_hbm,
    received_hbm,
    power_hbm,
    noise_hbm,
    gain_hbm,
    cluster_hbm,
    serving_hbm,
    owner_hbm,
    table_hbm,
    share_ref,
    rank_ref,
    coef_all,
    solved_all,
    wrow_ref,
    received_ref,
    power_ref,
    noise_ref,
    gain_ref,
    cluster_ref,
    serving_ref,
    owner_ref,
    solved_wide,
    guess,
    table,
    half,
    other,
    coef_send,
    coef_b,
    gains,
    pick,
    power_wide,
    smooth,
    cov,
    own,
    guess_sem,
    table_sem,
    half_send_sem,
    half_recv_sem,
    gain_send_sem,
    gain_recv_sem,
    coef_send_sem,
    coef_recv_sem,
    ring_send_sem,
    ring_recv_sem,
    local_sem,
    small_sem,
):
    stations, antennas, _, users, tones = guess.shape
    pieces = stations * antennas
    block = PEER_MAX * CU
    clusters = serving_ref.shape[0]
    me = lax.axis_index("ap")
    part = lax.axis_index("sc")
    node, place = ring_of
    spot = place(me)
    right = node(lax.rem(spot + 1, n))
    left = node(lax.rem(spot + n - 1, n))

    table_copy = pltpu.make_async_copy(table_hbm.at[part], table, table_sem)
    table_copy.start()
    small_copies = []
    for source, into in (
        (cluster_hbm, cluster_ref),
        (serving_hbm, serving_ref),
        (owner_hbm, owner_ref),
        (power_hbm, power_ref),
        (gain_hbm, gain_ref),
        (noise_hbm, noise_ref),
        (received_hbm, received_ref),
    ):
        copy = pltpu.make_async_copy(source, into, small_sem.at[len(small_copies)])
        copy.start()
        small_copies.append(copy)
    guess_copies = []
    for q in range(pieces):
        a, i = q // antennas, q % antennas
        copy = pltpu.make_async_copy(guess_hbm.at[a, i], guess.at[a, i], guess_sem.at[q])
        copy.start()
        guess_copies.append(copy)

    barrier = pltpu.get_barrier_semaphore()
    pl.semaphore_signal(barrier, inc=1, device_id={"sc": 1 - part}, device_id_type=MESH)
    for k in range(1, n):
        pl.semaphore_signal(
            barrier, inc=1, device_id={"ap": lax.rem(me + k, n)}, device_id_type=MESH
        )

    for copy in small_copies:
        copy.wait()
    owner_u, rank_u, served_u, before_u, serve_u, position = user_tables(
        cluster_ref[...], serving_ref[...], owner_ref[...], clusters, users, stations, n
    )
    mef = me.astype(jnp.float32)
    mine = iota((n, users), 0) == mef
    served_me = jnp.sum(jnp.where(mine, served_u, 0.0), axis=0, keepdims=True)
    before_me = jnp.sum(jnp.where(mine, before_u, 0.0), axis=0, keepdims=True)
    target = jnp.where(
        served_me > 0.5, owner_u * block + before_me * CU + position, -1.0
    )
    pick[...] = jnp.where(iota((n * block, users), 0) == target, 1.0, 0.0).astype(jnp.bfloat16)
    wide = jnp.broadcast_to(power_ref[...] * (1.0 / users), (LANES, users))
    power_wide[...] = jnp.transpose(wide)

    pl.semaphore_wait(barrier, n)

    gain_copies = []
    for k in range(1, n):
        peer = lax.rem(me + k, n)
        copy = pltpu.make_async_remote_copy(
            src_ref=gain_ref,
            dst_ref=gains.at[me],
            send_sem=gain_send_sem.at[k],
            recv_sem=gain_recv_sem.at[n - k],
            device_id={"ap": peer},
            device_id_type=MESH,
        )
        copy.start()
        gain_copies.append(copy)
    gains[me] = gain_ref[...]

    table_copy.wait()
    half_copies = []
    contract = (((1,), (1,)), ((), ()))
    for q in range(pieces):
        a, i = q // antennas, q % antennas
        guess_copies[q].wait()
        sums = lax.dot_general(
            guess[a, i, 0], table[:, :tones], contract, preferred_element_type=jnp.float32
        ) + lax.dot_general(
            guess[a, i, 1], table[:, tones:], contract, preferred_element_type=jnp.float32
        )
        half[q] = (sums * (1.0 / TONE_NUMBER)).astype(jnp.bfloat16)
        copy = pltpu.make_async_remote_copy(
            src_ref=half.at[q],
            dst_ref=other.at[q],
            send_sem=half_send_sem.at[q],
            recv_sem=half_recv_sem.at[q],
            device_id={"sc": 1 - part},
            device_id_type=MESH,
        )
        copy.start()
        half_copies.append(copy)
    for q in range(pieces):
        half_copies[q].wait_recv()
        total = (half[q].astype(jnp.float32) + other[q].astype(jnp.float32)).astype(jnp.bfloat16)
        coef_b[pl.ds(q * users, users), :] = total
        chosen = jnp.dot(pick[...], total, preferred_element_type=jnp.float32)
        coef_send[:, q] = chosen.astype(jnp.bfloat16).reshape(n, block, 2 * TAPS)
    coef_copies = []
    for k in range(1, n):
        peer = lax.rem(me + k, n)
        copy = pltpu.make_async_remote_copy(
            src_ref=coef_send.at[peer],
            dst_ref=coef_all.at[me],
            send_sem=coef_send_sem.at[k],
            recv_sem=coef_recv_sem.at[n - k],
            device_id={"ap": peer},
            device_id_type=MESH,
        )
        copy.start()
        coef_copies.append(copy)
    own_coef = pltpu.make_async_copy(coef_send.at[me], coef_all.at[me], local_sem)
    own_coef.start()

    width = tones // chunks
    symbols = received_ref.shape[3]
    rows = stations * symbols
    ring_copies = {}
    reach = {}
    for c in range(chunks):
        far, near = n // 2, n - 1 - n // 2
        reach[c] = (far, near) if c % 2 == 0 else (near, far)

    ready = []

    def origin_of(direction, step):
        back = lax.rem(spot + n - step, n) if direction == 0 else lax.rem(spot + step, n)
        return node(back)

    def ring_start(c, direction, step):
        if step > reach[c][direction]:
            return
        origin = origin_of(direction, step)
        source = own.at[c]
        if step > 0:
            ring_copies[c, direction, step - 1].wait_recv()
            source = solved_all.at[origin, c]
            ready.append((origin, c, source))
        if step == reach[c][direction]:
            return
        copy = pltpu.make_async_remote_copy(
            src_ref=source,
            dst_ref=solved_all.at[origin, c],
            send_sem=ring_send_sem.at[direction, c, step],
            recv_sem=ring_recv_sem.at[direction, c, step],
            device_id={"ap": right if direction == 0 else left},
            device_id_type=MESH,
        )
        copy.start()
        ring_copies[c, direction, step] = copy

    steps = max(max(r) for r in reach.values())
    entries = [(i, j) for i in range(antennas) for j in range(i + 1)]
    noise = jnp.concatenate(
        [
            jnp.broadcast_to(noise_ref[0:1, a : a + 1], (symbols, 1))
            for a in range(stations)
        ],
        axis=0,
    )
    for c in range(chunks):
        base = c * width
        for reim in range(2):
            columns = table[:, reim * tones + base : reim * tones + base + width]
            smooth[reim] = jnp.dot(coef_b[...], columns, preferred_element_type=jnp.float32)
        for a in range(stations):
            for l in range(width // LANES):
                lanes = pl.ds(l * LANES, LANES)

                def body(step, sums, a=a, lanes=lanes):
                    sums = list(sums)
                    for w in range(2):
                        row = (step * 2 + w) * 8
                        scale = power_wide[pl.ds(pl.multiple_of(row, 8), 8), :]
                        re, im = [], []
                        for i in range(antennas):
                            at = pl.multiple_of((a * antennas + i) * users + row, 8)
                            re.append(smooth[0, pl.ds(at, 8), lanes])
                            im.append(smooth[1, pl.ds(at, 8), lanes])
                        at = 0
                        for i in range(antennas):
                            sre, sim = re[i] * scale, im[i] * scale
                            for j in range(i + 1):
                                sums[at] = sums[at] + (sre * re[j] + sim * im[j])
                                at += 1
                                if j < i:
                                    sums[at] = sums[at] + (sim * re[j] - sre * im[j])
                                    at += 1
                    return tuple(sums)

                zero = jnp.zeros((8, LANES), jnp.float32)
                sums = lax.fori_loop(0, users // 16, body, (zero,) * (antennas * antennas))
                for e in range(antennas * antennas):
                    value = jnp.sum(sums[e], axis=0, keepdims=True)
                    cov[e, a * symbols : (a + 1) * symbols, lanes] = jnp.broadcast_to(
                        value, (symbols, LANES)
                    )
        cov_re = [[None] * antennas for _ in range(antennas)]
        cov_im = [[None] * antennas for _ in range(antennas)]
        at = 0
        for i, j in entries:
            cov_re[i][j] = cov[at]
            at += 1
            if i == j:
                cov_re[i][j] = cov_re[i][j] + noise
            else:
                cov_im[i][j] = cov[at]
                at += 1
        signal = []
        for i in range(antennas):
            signal.append(
                tuple(
                    jnp.concatenate(
                        [
                            received_ref[a, i, reim, :, base : base + width].astype(jnp.float32)
                            for a in range(stations)
                        ],
                        axis=0,
                    )
                    for reim in range(2)
                )
            )
        solved = hermitian_solve(cov_re, cov_im, signal)
        for i in range(antennas):
            joined = jnp.concatenate([solved[i][0], solved[i][1]], axis=0)
            own[c, pl.ds(i * 2 * rows, 2 * rows), :] = joined.astype(jnp.bfloat16)
        ready.append((me, c, own.at[c]))
        for d in range(c + 1):
            for direction in range(2):
                ring_start(d, direction, c - d)

    for copy in gain_copies:
        copy.wait_recv()
    weights = []
    totals = jnp.zeros((1, users), jnp.float32)
    for p in range(n):
        for a in range(stations):
            row = serve_u[p * stations + a : p * stations + a + 1] * gains[p, a : a + 1, :]
            weights.append(row)
            totals = totals + row
    scale = 1.0 / (1.0 + totals)
    for p in range(n):
        goal = jnp.where(
            (owner_u == mef) & (served_u[p : p + 1] > 0.5),
            before_u[p : p + 1] * CU + position,
            -1.0,
        )
        hits = iota((block, users), 0) == goal
        for a in range(stations):
            value = jnp.sum(
                jnp.where(hits, weights[p * stations + a] * scale, 0.0), axis=1, keepdims=True
            )
            wrow_ref[p, a] = jnp.broadcast_to(value, (block, LANES))
        for k in range(PEER_MAX):
            value = jnp.sum(
                jnp.where(hits[k * CU : k * CU + 1], rank_u, 0.0), axis=1, keepdims=True
            )
            rank_ref[p * PEER_MAX + k : p * PEER_MAX + k + 1, :] = jnp.broadcast_to(
                value, (1, LANES)
            ).astype(jnp.int32)


    for copy in coef_copies:
        copy.wait_recv()
    own_coef.wait()

    def combine(origin, c, source):
        base = c * width
        solved_wide[...] = source[...].astype(jnp.float32)
        coefs = coef_all[origin].reshape(pieces * block, 2 * TAPS)
        for reim in range(2):
            columns = table[:, reim * tones + base : reim * tones + base + width]
            smooth[reim, : pieces * block, :] = jnp.dot(
                coefs, columns, preferred_element_type=jnp.float32
            )

        def tile(l, carry):
            lanes = pl.ds(pl.multiple_of(l * LANES, LANES), LANES)
            sums = [[[None, None] for _ in range(symbols)] for _ in range(PEER_MAX)]
            for a in range(stations):
                weight = [wrow_ref[origin, a, pl.ds(k * CU, CU), :] for k in range(PEER_MAX)]
                for i in range(antennas):
                    re, im = [], []
                    for k in range(PEER_MAX):
                        at = (a * antennas + i) * block + k * CU
                        re.append(smooth[0, pl.ds(at, CU), lanes] * weight[k])
                        im.append(smooth[1, pl.ds(at, CU), lanes] * weight[k])
                    for s in range(symbols):
                        first = i * 2 * rows + a * symbols + s
                        sre = solved_wide[pl.ds(first, 1), lanes]
                        sim = solved_wide[pl.ds(first + rows, 1), lanes]
                        for k in range(PEER_MAX):
                            new_re = re[k] * sre + im[k] * sim
                            new_im = re[k] * sim - im[k] * sre
                            old = sums[k][s]
                            if old[0] is not None:
                                new_re, new_im = old[0] + new_re, old[1] + new_im
                            sums[k][s] = [new_re, new_im]
            for k in range(PEER_MAX):
                for s in range(symbols):
                    for reim in range(2):
                        share_ref[
                            c * (width // LANES) + l,
                            origin * PEER_MAX + k,
                            pl.ds((s * 2 + reim) * CU, CU),
                            :,
                        ] = sums[k][s][reim]
            return carry

        lax.fori_loop(0, width // LANES, tile, 0)

    def drain(most):
        for _ in range(most):
            if ready:
                combine(*ready.pop(0))

    drain(2)
    for late in range(chunks, chunks + steps + 1):
        for d in range(chunks):
            for direction in range(2):
                if late - d > 0:
                    ring_start(d, direction, late - d)
            drain(2)
    drain(len(ready))

    for copy in half_copies:
        copy.wait_send()
    for copy in gain_copies:
        copy.wait_send()
    for copy in coef_copies:
        copy.wait_send()
    for copy in ring_copies.values():
        copy.wait_send()


def second_kernel(n, rank_ref, share_ref, out_hbm, total, moved, out_sem):
    tiles, _, rows, _ = share_ref.shape
    pairs = rows // (2 * CU)
    height = CU * pairs * tiles * 2
    total[...] = jnp.zeros_like(total)
    slots = [rank_ref[k, 0] for k in range(n * PEER_MAX)]

    def tile(l, carry):
        for k in range(n * PEER_MAX):
            total[l, slots[k]] += share_ref[l, k]
        return carry

    lax.fori_loop(0, tiles, tile, 0)
    copies = []
    for r in range(OWN_MAX):

        def move(l, carry, r=r):
            for s in range(pairs):
                for reim in range(2):
                    moved[pl.ds(r * height + (s * tiles + l) * 2 + reim, CU, stride=pairs * tiles * 2), :] = (
                        total[l, r, pl.ds((s * 2 + reim) * CU, CU), :]
                    )
            return carry

        lax.fori_loop(0, tiles, move, 0)
        part = pl.ds(r * height, height)
        copy = pltpu.make_async_copy(moved.at[part], out_hbm.at[part], out_sem.at[r])
        copy.start()
        copies.append(copy)
    for copy in copies:
        copy.wait()


def ring_functions(mesh):
    n = mesh.shape["ap"]
    half = n // 2

    def plain(q):
        return q

    def node(q):
        upper = q // half
        return (1 - upper) * 2 * q + upper * (2 * (n - q) - 1)

    def place(d):
        odd = d % 2
        return (1 - odd) * (d // 2) + odd * (n - (d + 1) // 2)

    if n % 2:
        return plain, plain
    try:
        axes = list(mesh.axis_names)
        line = np.moveaxis(mesh.devices, axes.index("ap"), 0).reshape(n, -1)[:, 0]
        spots = [tuple(d.coords) for d in line]
        sizes = [max(s[x] for s in spots) + 1 for x in range(3)]

        def length(order):
            far = 0
            for q in range(n):
                one, two = spots[order(q)], spots[order((q + 1) % n)]
                far += sum(
                    min(abs(one[x] - two[x]), sizes[x] - abs(one[x] - two[x])) for x in range(3)
                )
            return far

        if length(plain) < length(node):
            return plain, plain
    except (AttributeError, TypeError):
        pass
    return node, place


def local(
    n,
    parts,
    ring_of,
    unsmoothed_link_guesses,
    received,
    user_power,
    noise_power,
    ap_gain,
    user_cluster,
    serving,
    cluster_owner,
):
    stations, antennas, _, users, tones = unsmoothed_link_guesses.shape
    symbols = received.shape[3]
    pieces = stations * antennas
    block = PEER_MAX * CU
    rows = stations * symbols
    chunks = 4
    width = tones // chunks
    steps = n // 2
    table = jnp.asarray(delay_tables(parts, tones))
    vmem = pl.BlockSpec(memory_space=pltpu.VMEM)
    smem = pl.BlockSpec(memory_space=pltpu.SMEM)
    anywhere = pl.BlockSpec(memory_space=pl.ANY)
    dma = pltpu.SemaphoreType.DMA
    bf16, f32 = jnp.bfloat16, jnp.float32
    hbm = pl.BlockSpec(memory_space=pltpu.HBM)
    tiles = tones // LANES
    share, rank = pl.pallas_call(
        functools.partial(first_kernel, n, chunks, ring_of),
        out_shape=(
            jax.ShapeDtypeStruct((tiles, n * PEER_MAX, symbols * 2 * CU, LANES), f32),
            jax.ShapeDtypeStruct((n * PEER_MAX, LANES), jnp.int32),
        ),
        in_specs=[hbm] * 9,
        out_specs=(vmem, vmem),
        scratch_shapes=[
            pltpu.VMEM((n, pieces, block, 2 * TAPS), bf16),
            pltpu.VMEM((n, chunks, antennas * 2 * rows, width), bf16),
            pltpu.VMEM((n, stations, block, LANES), f32),
            pltpu.VMEM(received.shape, bf16),
            pltpu.VMEM((1, users), f32),
            pltpu.VMEM((1, stations), f32),
            pltpu.VMEM((stations, users), f32),
            pltpu.VMEM((1, users), jnp.int32),
            pltpu.VMEM(serving.shape, jnp.int32),
            pltpu.VMEM((1, serving.shape[0]), jnp.int32),
            pltpu.VMEM((antennas * 2 * rows, width), f32),
            pltpu.VMEM((stations, antennas, 2, users, tones), bf16),
            pltpu.VMEM((2 * TAPS, 2 * tones), bf16),
            pltpu.VMEM((pieces, users, 2 * TAPS), bf16),
            pltpu.VMEM((pieces, users, 2 * TAPS), bf16),
            pltpu.VMEM((n, pieces, block, 2 * TAPS), bf16),
            pltpu.VMEM((pieces * users, 2 * TAPS), bf16),
            pltpu.VMEM((n, stations, users), f32),
            pltpu.VMEM((n * block, users), bf16),
            pltpu.VMEM((users, LANES), f32),
            pltpu.VMEM((2, pieces * users, width), f32),
            pltpu.VMEM((antennas * antennas, rows, width), f32),
            pltpu.VMEM((chunks, antennas * 2 * rows, width), bf16),
            dma((pieces,)),
            dma,
            dma((pieces,)),
            dma((pieces,)),
            dma((n,)),
            dma((n,)),
            dma((n,)),
            dma((n,)),
            dma((2, chunks, steps)),
            dma((2, chunks, steps)),
            dma,
            dma((7,)),
        ],
        compiler_params=pltpu.CompilerParams(
            collective_id=0, has_side_effects=True, vmem_limit_bytes=40 * 1024 * 1024
        ),
        name="smooth_solve_combine",
    )(
        unsmoothed_link_guesses,
        received,
        user_power.reshape(1, users),
        noise_power.reshape(1, stations),
        ap_gain,
        user_cluster.reshape(1, users),
        serving,
        cluster_owner.reshape(1, -1),
        table,
    )
    lines = OWN_MAX * CU * symbols * tiles * 2
    placed = pl.pallas_call(
        functools.partial(second_kernel, n),
        out_shape=jax.ShapeDtypeStruct((lines, LANES), f32),
        in_specs=[smem, vmem],
        out_specs=hbm,
        scratch_shapes=[
            pltpu.VMEM((tiles, OWN_MAX, symbols * 2 * CU, LANES), f32),
            pltpu.VMEM((lines, LANES), f32),
            dma((OWN_MAX,)),
        ],
        compiler_params=pltpu.CompilerParams(vmem_limit_bytes=16 * 1024 * 1024),
        name="place",
    )(rank, share)
    placed = placed.reshape(OWN_MAX, CU, symbols, tiles, 2, LANES)
    placed = jnp.transpose(placed, (0, 1, 2, 4, 3, 5))
    return placed.reshape(OWN_MAX, CU, symbols, 2, tones)


def solution(mesh):
    placed = (
        P(("cell", "ap"), None, None, None, "sc"),
        P(("cell", "ap"), None, None, None, "sc"),
        P("cell"),
        P(("cell", "ap")),
        P(("cell", "ap"), None),
        P("cell"),
        P("cell", None),
        P("cell", None),
    )
    return jax.shard_map(
        functools.partial(local, mesh.shape["ap"], mesh.shape["sc"], ring_functions(mesh)),
        mesh=mesh,
        in_specs=placed,
        out_specs=P(("cell", "ap"), None, None, None, "sc"),
        check_vma=False,
    )
```

```python
import functools
import math

import jax
import jax.numpy as jnp
import numpy as np
from jax import lax
from jax.experimental import pallas as pl
from jax.experimental.pallas import tpu as pltpu
from jax.sharding import PartitionSpec as P

TONE_NUMBER = 2048
TAPS = 64
CU = 8
OWN_MAX = 4
PEER_MAX = 2
MESH = pl.DeviceIdType.MESH
LANES = 128
VMEM_BYTES = 67043328


def complex_times(left_factor, right_factor):
    return (
        left_factor[0] * right_factor[0] - left_factor[1] * right_factor[1],
        left_factor[0] * right_factor[1] + left_factor[1] * right_factor[0],
    )


def times_conj(left_factor, right_factor):
    return (
        left_factor[0] * right_factor[0] + left_factor[1] * right_factor[1],
        left_factor[1] * right_factor[0] - left_factor[0] * right_factor[1],
    )


def hermitian_solve(cov_re, cov_im, right):
    dimension = len(cov_re)
    factor = {}
    inverses = []
    for j in range(dimension):
        pivot = cov_re[j][j]
        for k in range(j):
            element = factor[j, k]
            pivot = pivot - (element[0] * element[0] + element[1] * element[1])
        inverse = 1.0 / jnp.sqrt(pivot)
        inverses.append(inverse)
        for i in range(j + 1, dimension):
            running = (cov_re[i][j], cov_im[i][j])
            for k in range(j):
                product = times_conj(factor[i, k], factor[j, k])
                running = (running[0] - product[0], running[1] - product[1])
            factor[i, j] = (running[0] * inverse, running[1] * inverse)
    forward = []
    for i in range(dimension):
        running = right[i]
        for k in range(i):
            product = complex_times(factor[i, k], forward[k])
            running = (running[0] - product[0], running[1] - product[1])
        forward.append((running[0] * inverses[i], running[1] * inverses[i]))
    result = [None] * dimension
    for i in range(dimension - 1, -1, -1):
        running = forward[i]
        for k in range(i + 1, dimension):
            product = times_conj(result[k], factor[k, i])
            running = (running[0] - product[0], running[1] - product[1])
        result[i] = (running[0] * inverses[i], running[1] * inverses[i])
    return result


def delay_tables(parts, tones):
    made = []
    for part in range(parts):
        values = part * tones + np.arange(tones, dtype=np.int32)
        rotation = np.arange(TAPS, dtype=np.int32)[:, None] * values[None, :] % TONE_NUMBER
        angles = rotation.astype(np.float32) * np.float32(2.0 * math.pi / TONE_NUMBER)
        cosine, sine = np.cos(angles), np.sin(angles)
        made.append(
            np.concatenate(
                [
                    np.concatenate([cosine, sine], axis=0),
                    np.concatenate([-sine, cosine], axis=0),
                ],
                axis=1,
            )
        )
    return np.stack(made).astype(jnp.bfloat16)


def exact_dot(left, right, dims):
    return lax.dot_general(
        left.astype(jnp.bfloat16),
        right.astype(jnp.bfloat16),
        (dims, ((), ())),
        preferred_element_type=jnp.float32,
    )


def iota(shape, dim):
    return lax.broadcasted_iota(jnp.int32, shape, dim).astype(jnp.float32)


def user_tables(user_cluster, serving, owner, clusters, users, group, n):
    onehot = (iota((clusters, users), 0) == user_cluster.astype(jnp.float32)).astype(jnp.float32)
    owner_row = owner.astype(jnp.float32)
    square = (clusters, clusters)
    rows, cols = iota(square, 0), iota(square, 1)
    owner_col = jnp.sum(jnp.where(rows == cols, owner_row, 0.0), axis=1, keepdims=True)
    same = owner_col == owner_row
    earlier = jnp.where(same & (cols < rows), 1.0, 0.0)
    serve = serving.astype(jnp.float32)
    pair = jnp.where(
        jnp.floor((iota((group * n, n), 0) + 0.5) * (1.0 / group)) == iota((group * n, n), 1),
        1.0,
        0.0,
    )
    served = jnp.where(exact_dot(serve, pair, ((1,), (0,))) > 0.5, 1.0, 0.0)
    before = exact_dot(earlier, served, ((1,), (0,)))
    rank = jnp.sum(earlier, axis=1, keepdims=True)
    owner_u = jnp.sum(onehot * owner_col, axis=0, keepdims=True)
    rank_u = jnp.sum(onehot * rank, axis=0, keepdims=True)
    served_u = exact_dot(served, onehot, ((0,), (0,)))
    before_u = exact_dot(before, onehot, ((0,), (0,)))
    serve_u = exact_dot(serve, onehot, ((0,), (0,)))
    equal = exact_dot(onehot, onehot, ((0,), (0,)))
    both = (users, users)
    position = jnp.sum(
        jnp.where(iota(both, 0) < iota(both, 1), equal, 0.0), axis=0, keepdims=True
    )
    return owner_u, rank_u, served_u, before_u, serve_u, position


def first_kernel(
    n,
    chunks,
    ring_of,
    guess_hbm,
    received_hbm,
    power_hbm,
    noise_hbm,
    gain_hbm,
    cluster_hbm,
    serving_hbm,
    owner_hbm,
    table_hbm,
    share_hbm,
    rank_hbm,
    share_ref,
    rank_ref,
    coef_all,
    solved_all,
    wrow_ref,
    received_ref,
    power_ref,
    noise_ref,
    gain_ref,
    cluster_ref,
    serving_ref,
    owner_ref,
    solved_wide,
    guess,
    table,
    half,
    other,
    coef_send,
    coef_b,
    gains,
    pick,
    power_wide,
    smooth,
    cov,
    own,
    guess_sem,
    table_sem,
    half_send_sem,
    half_recv_sem,
    gain_send_sem,
    gain_recv_sem,
    coef_send_sem,
    coef_recv_sem,
    ring_send_sem,
    ring_recv_sem,
    local_sem,
    small_sem,
    relay_send_sem,
    relay_recv_sem,
    share_sem,
    rank_sem,
):
    stations, antennas, _, users, tones = guess.shape
    pieces = stations * antennas
    block = PEER_MAX * CU
    clusters = serving_ref.shape[0]
    me = lax.axis_index("ap")
    part = lax.axis_index("sc")
    node, place = ring_of
    spot = place(me)
    right = node(lax.rem(spot + 1, n))
    left = node(lax.rem(spot + n - 1, n))

    table_copy = pltpu.make_async_copy(table_hbm.at[part], table, table_sem)
    table_copy.start()
    small_copies = []
    for source, into in (
        (cluster_hbm, cluster_ref),
        (serving_hbm, serving_ref),
        (owner_hbm, owner_ref),
        (power_hbm, power_ref),
        (gain_hbm, gain_ref),
        (noise_hbm, noise_ref),
        (received_hbm, received_ref),
    ):
        copy = pltpu.make_async_copy(source, into, small_sem.at[len(small_copies)])
        copy.start()
        small_copies.append(copy)
    guess_copies = []
    for q in range(pieces):
        a, i = q // antennas, q % antennas
        copy = pltpu.make_async_copy(guess_hbm.at[a, i], guess.at[a, i], guess_sem.at[q])
        copy.start()
        guess_copies.append(copy)

    barrier = pltpu.get_barrier_semaphore()
    pl.semaphore_signal(barrier, inc=1, device_id={"sc": 1 - part}, device_id_type=MESH)
    for k in range(1, n):
        pl.semaphore_signal(
            barrier, inc=1, device_id={"ap": lax.rem(me + k, n)}, device_id_type=MESH
        )

    for copy in small_copies:
        copy.wait()
    owner_u, rank_u, served_u, before_u, serve_u, position = user_tables(
        cluster_ref[...], serving_ref[...], owner_ref[...], clusters, users, stations, n
    )
    mef = me.astype(jnp.float32)
    mine = iota((n, users), 0) == mef
    served_me = jnp.sum(jnp.where(mine, served_u, 0.0), axis=0, keepdims=True)
    before_me = jnp.sum(jnp.where(mine, before_u, 0.0), axis=0, keepdims=True)
    target = jnp.where(
        served_me > 0.5, owner_u * block + before_me * CU + position, -1.0
    )
    pick[...] = jnp.where(iota((n * block, users), 0) == target, 1.0, 0.0).astype(jnp.bfloat16)
    wide = jnp.broadcast_to(power_ref[...] * (1.0 / users), (LANES, users))
    power_wide[...] = jnp.transpose(wide)

    pl.semaphore_wait(barrier, n)

    gain_copies = []
    for k in range(1, n):
        peer = lax.rem(me + k, n)
        copy = pltpu.make_async_remote_copy(
            src_ref=gain_ref,
            dst_ref=gains.at[me],
            send_sem=gain_send_sem.at[k],
            recv_sem=gain_recv_sem.at[n - k],
            device_id={"ap": peer},
            device_id_type=MESH,
        )
        copy.start()
        gain_copies.append(copy)
    gains[me] = gain_ref[...]

    table_copy.wait()
    half_copies = []
    contract = (((1,), (1,)), ((), ()))
    for q in range(pieces):
        a, i = q // antennas, q % antennas
        guess_copies[q].wait()
        sums = lax.dot_general(
            guess[a, i, 0], table[:, :tones], contract, preferred_element_type=jnp.float32
        ) + lax.dot_general(
            guess[a, i, 1], table[:, tones:], contract, preferred_element_type=jnp.float32
        )
        half[q] = (sums * (1.0 / TONE_NUMBER)).astype(jnp.bfloat16)
        copy = pltpu.make_async_remote_copy(
            src_ref=half.at[q],
            dst_ref=other.at[q],
            send_sem=half_send_sem.at[q],
            recv_sem=half_recv_sem.at[q],
            device_id={"sc": 1 - part},
            device_id_type=MESH,
        )
        copy.start()
        half_copies.append(copy)
    for q in range(pieces):
        half_copies[q].wait_recv()
        total = (half[q].astype(jnp.float32) + other[q].astype(jnp.float32)).astype(jnp.bfloat16)
        coef_b[pl.ds(q * users, users), :] = total
        chosen = jnp.dot(pick[...], total, preferred_element_type=jnp.float32)
        coef_send[:, q] = chosen.astype(jnp.bfloat16).reshape(n, block, 2 * TAPS)
    coef_copies = []
    mine_half = pl.ds(part * (pieces // 2), pieces // 2)
    for k in range(1, n):
        peer = lax.rem(me + k, n)
        copy = pltpu.make_async_remote_copy(
            src_ref=coef_send.at[peer, mine_half],
            dst_ref=coef_all.at[me, mine_half],
            send_sem=coef_send_sem.at[k],
            recv_sem=coef_recv_sem.at[n - k],
            device_id={"ap": peer},
            device_id_type=MESH,
        )
        copy.start()
        coef_copies.append(copy)
    own_coef = pltpu.make_async_copy(coef_send.at[me], coef_all.at[me], local_sem)
    own_coef.start()

    width = tones // chunks
    symbols = received_ref.shape[3]
    rows = stations * symbols
    ring_copies = {}
    reach = {}
    for c in range(chunks):
        far, near = n // 2, n - 1 - n // 2
        reach[c] = (far, near) if c % 2 == 0 else (near, far)

    ready = []

    def origin_of(direction, step):
        back = lax.rem(spot + n - step, n) if direction == 0 else lax.rem(spot + step, n)
        return node(back)

    def ring_start(c, direction, step):
        if step > reach[c][direction]:
            return
        origin = origin_of(direction, step)
        source = own.at[c]
        if step > 0:
            ring_copies[c, direction, step - 1].wait_recv()
            source = solved_all.at[origin, c]
            ready.append((origin, c, source))
        if step == reach[c][direction]:
            return
        copy = pltpu.make_async_remote_copy(
            src_ref=source,
            dst_ref=solved_all.at[origin, c],
            send_sem=ring_send_sem.at[direction, c, step],
            recv_sem=ring_recv_sem.at[direction, c, step],
            device_id={"ap": right if direction == 0 else left},
            device_id_type=MESH,
        )
        copy.start()
        ring_copies[c, direction, step] = copy

    steps = max(max(r) for r in reach.values())
    entries = [(i, j) for i in range(antennas) for j in range(i + 1)]
    noise = jnp.concatenate(
        [
            jnp.broadcast_to(noise_ref[0:1, a : a + 1], (symbols, 1))
            for a in range(stations)
        ],
        axis=0,
    )
    for c in range(chunks):
        base = c * width
        for reim in range(2):
            columns = table[:, reim * tones + base : reim * tones + base + width]
            smooth[reim] = jnp.dot(coef_b[...], columns, preferred_element_type=jnp.float32)
        for a in range(stations):
            for l in range(width // LANES):
                lanes = pl.ds(l * LANES, LANES)

                def body(step, sums, a=a, lanes=lanes):
                    sums = list(sums)
                    for w in range(2):
                        row = (step * 2 + w) * 8
                        scale = power_wide[pl.ds(pl.multiple_of(row, 8), 8), :]
                        re, im = [], []
                        for i in range(antennas):
                            at = pl.multiple_of((a * antennas + i) * users + row, 8)
                            re.append(smooth[0, pl.ds(at, 8), lanes])
                            im.append(smooth[1, pl.ds(at, 8), lanes])
                        at = 0
                        for i in range(antennas):
                            sre, sim = re[i] * scale, im[i] * scale
                            for j in range(i + 1):
                                sums[at] = sums[at] + (sre * re[j] + sim * im[j])
                                at += 1
                                if j < i:
                                    sums[at] = sums[at] + (sim * re[j] - sre * im[j])
                                    at += 1
                    return tuple(sums)

                zero = jnp.zeros((8, LANES), jnp.float32)
                sums = lax.fori_loop(0, users // 16, body, (zero,) * (antennas * antennas))
                for e in range(antennas * antennas):
                    value = jnp.sum(sums[e], axis=0, keepdims=True)
                    cov[e, a * symbols : (a + 1) * symbols, lanes] = jnp.broadcast_to(
                        value, (symbols, LANES)
                    )
        cov_re = [[None] * antennas for _ in range(antennas)]
        cov_im = [[None] * antennas for _ in range(antennas)]
        at = 0
        for i, j in entries:
            cov_re[i][j] = cov[at]
            at += 1
            if i == j:
                cov_re[i][j] = cov_re[i][j] + noise
            else:
                cov_im[i][j] = cov[at]
                at += 1
        signal = []
        for i in range(antennas):
            signal.append(
                tuple(
                    jnp.concatenate(
                        [
                            received_ref[a, i, reim, :, base : base + width].astype(jnp.float32)
                            for a in range(stations)
                        ],
                        axis=0,
                    )
                    for reim in range(2)
                )
            )
        solved = hermitian_solve(cov_re, cov_im, signal)
        for i in range(antennas):
            joined = jnp.concatenate([solved[i][0], solved[i][1]], axis=0)
            own[c, pl.ds(i * 2 * rows, 2 * rows), :] = joined.astype(jnp.bfloat16)
        ready.append((me, c, own.at[c]))
        for d in range(c + 1):
            for direction in range(2):
                ring_start(d, direction, c - d)

    for copy in gain_copies:
        copy.wait_recv()
    weights = []
    totals = jnp.zeros((1, users), jnp.float32)
    for p in range(n):
        for a in range(stations):
            row = serve_u[p * stations + a : p * stations + a + 1] * gains[p, a : a + 1, :]
            weights.append(row)
            totals = totals + row
    scale = 1.0 / (1.0 + totals)
    for p in range(n):
        goal = jnp.where(
            (owner_u == mef) & (served_u[p : p + 1] > 0.5),
            before_u[p : p + 1] * CU + position,
            -1.0,
        )
        hits = iota((block, users), 0) == goal
        for a in range(stations):
            value = jnp.sum(
                jnp.where(hits, weights[p * stations + a] * scale, 0.0), axis=1, keepdims=True
            )
            wrow_ref[p, a] = jnp.broadcast_to(value, (block, LANES))
        for k in range(PEER_MAX):
            value = jnp.sum(
                jnp.where(hits[k * CU : k * CU + 1], rank_u, 0.0), axis=1, keepdims=True
            )
            rank_ref[p * PEER_MAX + k : p * PEER_MAX + k + 1, :] = jnp.broadcast_to(
                value, (1, LANES)
            ).astype(jnp.int32)


    rank_copy = pltpu.make_async_copy(rank_ref, rank_hbm, rank_sem)
    rank_copy.start()
    relay_copies = []
    for k in range(1, n):
        coef_copies[n - k - 1].wait_recv()
        origin = lax.rem(me + n - (n - k), n)
        copy = pltpu.make_async_remote_copy(
            src_ref=coef_all.at[origin, mine_half],
            dst_ref=coef_all.at[origin, mine_half],
            send_sem=relay_send_sem.at[k],
            recv_sem=relay_recv_sem.at[k],
            device_id={"sc": 1 - part},
            device_id_type=MESH,
        )
        copy.start()
        relay_copies.append(copy)
    own_coef.wait()
    share_copies = []

    def combine(origin, c, source):
        base = c * width
        solved_wide[...] = source[...].astype(jnp.float32)
        coefs = coef_all[origin].reshape(pieces * block, 2 * TAPS)
        for reim in range(2):
            columns = table[:, reim * tones + base : reim * tones + base + width]
            smooth[reim, : pieces * block, :] = jnp.dot(
                coefs, columns, preferred_element_type=jnp.float32
            )

        def tile(l, carry):
            lanes = pl.ds(pl.multiple_of(l * LANES, LANES), LANES)
            sums = [[[None, None] for _ in range(symbols)] for _ in range(PEER_MAX)]
            for a in range(stations):
                weight = [wrow_ref[origin, a, pl.ds(k * CU, CU), :] for k in range(PEER_MAX)]
                for i in range(antennas):
                    re, im = [], []
                    for k in range(PEER_MAX):
                        at = (a * antennas + i) * block + k * CU
                        re.append(smooth[0, pl.ds(at, CU), lanes] * weight[k])
                        im.append(smooth[1, pl.ds(at, CU), lanes] * weight[k])
                    for s in range(symbols):
                        first = i * 2 * rows + a * symbols + s
                        sre = solved_wide[pl.ds(first, 1), lanes]
                        sim = solved_wide[pl.ds(first + rows, 1), lanes]
                        for k in range(PEER_MAX):
                            new_re = re[k] * sre + im[k] * sim
                            new_im = re[k] * sim - im[k] * sre
                            old = sums[k][s]
                            if old[0] is not None:
                                new_re, new_im = old[0] + new_re, old[1] + new_im
                            sums[k][s] = [new_re, new_im]
            for k in range(PEER_MAX):
                for s in range(symbols):
                    for reim in range(2):
                        share_ref[
                            c * (width // LANES) + l,
                            origin * PEER_MAX + k,
                            pl.ds((s * 2 + reim) * CU, CU),
                            :,
                        ] = sums[k][s][reim]
            return carry

        lax.fori_loop(0, width // LANES, tile, 0)
        place = (
            pl.ds(c * (width // LANES), width // LANES),
            pl.ds(origin * PEER_MAX, PEER_MAX),
        )
        copy = pltpu.make_async_copy(
            share_ref.at[place], share_hbm.at[place], share_sem.at[len(share_copies)]
        )
        copy.start()
        share_copies.append(copy)

    def drain(most):
        for _ in range(most):
            if ready:
                combine(*ready.pop(0))

    late_slots = range(chunks, chunks + steps)
    for late in late_slots:
        for d in range(chunks):
            for direction in range(2):
                if late - d > 0:
                    ring_start(d, direction, late - d)
        if late == chunks:
            for copy in relay_copies:
                copy.wait_recv()
        drain(-(-n * chunks // (steps + 1)))
    drain(len(ready))
    rank_copy.wait()
    for copy in share_copies:
        copy.wait()
    for copy in relay_copies:
        copy.wait_send()
    for copy in half_copies:
        copy.wait_send()
    for copy in gain_copies:
        copy.wait_send()
    for copy in coef_copies:
        copy.wait_send()
    for copy in ring_copies.values():
        copy.wait_send()


def second_kernel(n, rank_ref, share_ref, out_hbm, total, moved, out_sem):
    _, _, rows, _ = share_ref.shape
    pairs = rows // (2 * CU)
    tiles = pl.num_programs(0)
    l = pl.program_id(0)
    stride = moved.shape[0] // (OWN_MAX * CU)
    height = CU * stride
    total[...] = jnp.zeros_like(total)
    for k in range(n * PEER_MAX):
        total[rank_ref[k, 0]] += share_ref[0, k]
    for r in range(OWN_MAX):
        for s in range(pairs):
            for reim in range(2):
                first = r * height + (s * tiles + l) * 2 + reim
                moved[pl.ds(first, CU, stride=stride), :] = total[
                    r, pl.ds((s * 2 + reim) * CU, CU), :
                ]

    @pl.when(l == tiles - 1)
    def _():
        copy = pltpu.make_async_copy(moved, out_hbm, out_sem)
        copy.start()
        copy.wait()


def ring_functions(mesh):
    n = mesh.shape["ap"]
    half = n // 2

    def plain(q):
        return q

    def node(q):
        upper = q // half
        return (1 - upper) * 2 * q + upper * (2 * (n - q) - 1)

    def place(d):
        odd = d % 2
        return (1 - odd) * (d // 2) + odd * (n - (d + 1) // 2)

    if n % 2:
        return plain, plain
    try:
        axes = list(mesh.axis_names)
        line = np.moveaxis(mesh.devices, axes.index("ap"), 0).reshape(n, -1)[:, 0]
        spots = [tuple(d.coords) for d in line]
        sizes = [max(s[x] for s in spots) + 1 for x in range(3)]

        def length(order):
            far = 0
            for q in range(n):
                one, two = spots[order(q)], spots[order((q + 1) % n)]
                far += sum(
                    min(abs(one[x] - two[x]), sizes[x] - abs(one[x] - two[x])) for x in range(3)
                )
            return far

        if length(plain) < length(node):
            return plain, plain
    except (AttributeError, TypeError):
        pass
    return node, place


def local(
    n,
    parts,
    ring_of,
    unsmoothed_link_guesses,
    received,
    user_power,
    noise_power,
    ap_gain,
    user_cluster,
    serving,
    cluster_owner,
):
    stations, antennas, _, users, tones = unsmoothed_link_guesses.shape
    symbols = received.shape[3]
    pieces = stations * antennas
    block = PEER_MAX * CU
    rows = stations * symbols
    chunks = 4
    width = tones // chunks
    steps = n // 2
    table = jnp.asarray(delay_tables(parts, tones))
    vmem = pl.BlockSpec(memory_space=pltpu.VMEM)
    smem = pl.BlockSpec(memory_space=pltpu.SMEM)
    anywhere = pl.BlockSpec(memory_space=pl.ANY)
    dma = pltpu.SemaphoreType.DMA
    bf16, f32 = jnp.bfloat16, jnp.float32
    hbm = pl.BlockSpec(memory_space=pltpu.HBM)
    tiles = tones // LANES
    share, rank = pl.pallas_call(
        functools.partial(first_kernel, n, chunks, ring_of),
        out_shape=(
            jax.ShapeDtypeStruct((tiles, n * PEER_MAX, symbols * 2 * CU, LANES), f32),
            jax.ShapeDtypeStruct((n * PEER_MAX, LANES), jnp.int32),
        ),
        in_specs=[hbm] * 9,
        out_specs=(hbm, hbm),
        scratch_shapes=[
            pltpu.VMEM((tiles, n * PEER_MAX, symbols * 2 * CU, LANES), f32),
            pltpu.VMEM((n * PEER_MAX, LANES), jnp.int32),
            pltpu.VMEM((n, pieces, block, 2 * TAPS), bf16),
            pltpu.VMEM((n, chunks, antennas * 2 * rows, width), bf16),
            pltpu.VMEM((n, stations, block, LANES), f32),
            pltpu.VMEM(received.shape, bf16),
            pltpu.VMEM((1, users), f32),
            pltpu.VMEM((1, stations), f32),
            pltpu.VMEM((stations, users), f32),
            pltpu.VMEM((1, users), jnp.int32),
            pltpu.VMEM(serving.shape, jnp.int32),
            pltpu.VMEM((1, serving.shape[0]), jnp.int32),
            pltpu.VMEM((antennas * 2 * rows, width), f32),
            pltpu.VMEM((stations, antennas, 2, users, tones), bf16),
            pltpu.VMEM((2 * TAPS, 2 * tones), bf16),
            pltpu.VMEM((pieces, users, 2 * TAPS), bf16),
            pltpu.VMEM((pieces, users, 2 * TAPS), bf16),
            pltpu.VMEM((n, pieces, block, 2 * TAPS), bf16),
            pltpu.VMEM((pieces * users, 2 * TAPS), bf16),
            pltpu.VMEM((n, stations, users), f32),
            pltpu.VMEM((n * block, users), bf16),
            pltpu.VMEM((users, LANES), f32),
            pltpu.VMEM((2, pieces * users, width), f32),
            pltpu.VMEM((antennas * antennas, rows, width), f32),
            pltpu.VMEM((chunks, antennas * 2 * rows, width), bf16),
            dma((pieces,)),
            dma,
            dma((pieces,)),
            dma((pieces,)),
            dma((n,)),
            dma((n,)),
            dma((n,)),
            dma((n,)),
            dma((2, chunks, steps)),
            dma((2, chunks, steps)),
            dma,
            dma((7,)),
            dma((n,)),
            dma((n,)),
            dma((n * chunks,)),
            dma,
        ],
        compiler_params=pltpu.CompilerParams(
            collective_id=0, has_side_effects=True, vmem_limit_bytes=VMEM_BYTES
        ),
        name="smooth_solve_combine",
    )(
        unsmoothed_link_guesses,
        received,
        user_power.reshape(1, users),
        noise_power.reshape(1, stations),
        ap_gain,
        user_cluster.reshape(1, users),
        serving,
        cluster_owner.reshape(1, -1),
        table,
    )
    lines = OWN_MAX * CU * symbols * tiles * 2
    placed = pl.pallas_call(
        functools.partial(second_kernel, n),
        out_shape=jax.ShapeDtypeStruct((lines, LANES), f32),
        grid=(tiles,),
        in_specs=[
            smem,
            pl.BlockSpec(
                (1, n * PEER_MAX, symbols * 2 * CU, LANES), lambda l: (l, 0, 0, 0)
            ),
        ],
        out_specs=hbm,
        scratch_shapes=[
            pltpu.VMEM((OWN_MAX, symbols * 2 * CU, LANES), f32),
            pltpu.VMEM((lines, LANES), f32),
            dma,
        ],
        compiler_params=pltpu.CompilerParams(vmem_limit_bytes=VMEM_BYTES),
        name="place",
    )(rank, share)
    placed = placed.reshape(OWN_MAX, CU, symbols, tiles, 2, LANES)
    placed = jnp.transpose(placed, (0, 1, 2, 4, 3, 5))
    return placed.reshape(OWN_MAX, CU, symbols, 2, tones)


def solution(mesh):
    placed = (
        P(("cell", "ap"), None, None, None, "sc"),
        P(("cell", "ap"), None, None, None, "sc"),
        P("cell"),
        P(("cell", "ap")),
        P(("cell", "ap"), None),
        P("cell"),
        P("cell", None),
        P("cell", None),
    )
    return jax.shard_map(
        functools.partial(local, mesh.shape["ap"], mesh.shape["sc"], ring_functions(mesh)),
        mesh=mesh,
        in_specs=placed,
        out_specs=P(("cell", "ap"), None, None, None, "sc"),
        check_vma=False,
    )
```

```python
import functools
import math

import jax
import jax.numpy as jnp
import numpy as np
from jax import lax
from jax.experimental import pallas as pl
from jax.experimental.pallas import tpu as pltpu
from jax.sharding import PartitionSpec as P

TONE_NUMBER = 2048
TAPS = 64
CU = 8
OWN_MAX = 4
PEER_MAX = 2
MESH = pl.DeviceIdType.MESH
LANES = 128
VMEM_BYTES = 67043328


def complex_times(left_factor, right_factor):
    return (
        left_factor[0] * right_factor[0] - left_factor[1] * right_factor[1],
        left_factor[0] * right_factor[1] + left_factor[1] * right_factor[0],
    )


def times_conj(left_factor, right_factor):
    return (
        left_factor[0] * right_factor[0] + left_factor[1] * right_factor[1],
        left_factor[1] * right_factor[0] - left_factor[0] * right_factor[1],
    )


def hermitian_solve(cov_re, cov_im, right):
    dimension = len(cov_re)
    factor = {}
    inverses = []
    for j in range(dimension):
        pivot = cov_re[j][j]
        for k in range(j):
            element = factor[j, k]
            pivot = pivot - (element[0] * element[0] + element[1] * element[1])
        inverse = 1.0 / jnp.sqrt(pivot)
        inverses.append(inverse)
        for i in range(j + 1, dimension):
            running = (cov_re[i][j], cov_im[i][j])
            for k in range(j):
                product = times_conj(factor[i, k], factor[j, k])
                running = (running[0] - product[0], running[1] - product[1])
            factor[i, j] = (running[0] * inverse, running[1] * inverse)
    forward = []
    for i in range(dimension):
        running = right[i]
        for k in range(i):
            product = complex_times(factor[i, k], forward[k])
            running = (running[0] - product[0], running[1] - product[1])
        forward.append((running[0] * inverses[i], running[1] * inverses[i]))
    result = [None] * dimension
    for i in range(dimension - 1, -1, -1):
        running = forward[i]
        for k in range(i + 1, dimension):
            product = times_conj(result[k], factor[k, i])
            running = (running[0] - product[0], running[1] - product[1])
        result[i] = (running[0] * inverses[i], running[1] * inverses[i])
    return result


def delay_tables(parts, tones):
    made = []
    for part in range(parts):
        values = part * tones + np.arange(tones, dtype=np.int32)
        rotation = np.arange(TAPS, dtype=np.int32)[:, None] * values[None, :] % TONE_NUMBER
        angles = rotation.astype(np.float32) * np.float32(2.0 * math.pi / TONE_NUMBER)
        cosine, sine = np.cos(angles), np.sin(angles)
        made.append(
            np.concatenate(
                [
                    np.concatenate([cosine, sine], axis=0),
                    np.concatenate([-sine, cosine], axis=0),
                ],
                axis=1,
            )
        )
    return np.stack(made).astype(jnp.bfloat16)


def exact_dot(left, right, dims):
    return lax.dot_general(
        left.astype(jnp.bfloat16),
        right.astype(jnp.bfloat16),
        (dims, ((), ())),
        preferred_element_type=jnp.float32,
    )


def iota(shape, dim):
    return lax.broadcasted_iota(jnp.int32, shape, dim).astype(jnp.float32)


def user_tables(user_cluster, serving, owner, clusters, users, group, n):
    onehot = (iota((clusters, users), 0) == user_cluster.astype(jnp.float32)).astype(jnp.float32)
    owner_row = owner.astype(jnp.float32)
    square = (clusters, clusters)
    rows, cols = iota(square, 0), iota(square, 1)
    owner_col = jnp.sum(jnp.where(rows == cols, owner_row, 0.0), axis=1, keepdims=True)
    same = owner_col == owner_row
    earlier = jnp.where(same & (cols < rows), 1.0, 0.0)
    serve = serving.astype(jnp.float32)
    pair = jnp.where(
        jnp.floor((iota((group * n, n), 0) + 0.5) * (1.0 / group)) == iota((group * n, n), 1),
        1.0,
        0.0,
    )
    served = jnp.where(exact_dot(serve, pair, ((1,), (0,))) > 0.5, 1.0, 0.0)
    before = exact_dot(earlier, served, ((1,), (0,)))
    rank = jnp.sum(earlier, axis=1, keepdims=True)
    owner_u = jnp.sum(onehot * owner_col, axis=0, keepdims=True)
    rank_u = jnp.sum(onehot * rank, axis=0, keepdims=True)
    served_u = exact_dot(served, onehot, ((0,), (0,)))
    before_u = exact_dot(before, onehot, ((0,), (0,)))
    serve_u = exact_dot(serve, onehot, ((0,), (0,)))
    equal = exact_dot(onehot, onehot, ((0,), (0,)))
    both = (users, users)
    position = jnp.sum(
        jnp.where(iota(both, 0) < iota(both, 1), equal, 0.0), axis=0, keepdims=True
    )
    return owner_u, rank_u, served_u, before_u, serve_u, position


def first_kernel(
    n,
    chunks,
    ring_of,
    guess_hbm,
    received_hbm,
    power_hbm,
    noise_hbm,
    gain_hbm,
    cluster_hbm,
    serving_hbm,
    owner_hbm,
    table_hbm,
    share_ref,
    rank_ref,
    coef_all,
    solved_all,
    wrow_ref,
    received_ref,
    power_ref,
    noise_ref,
    gain_ref,
    cluster_ref,
    serving_ref,
    owner_ref,
    solved_wide,
    guess,
    table,
    half,
    other,
    coef_send,
    coef_b,
    gains,
    pick,
    power_wide,
    smooth,
    cov,
    own,
    guess_sem,
    table_sem,
    half_send_sem,
    half_recv_sem,
    gain_send_sem,
    gain_recv_sem,
    coef_send_sem,
    coef_recv_sem,
    ring_send_sem,
    ring_recv_sem,
    local_sem,
    small_sem,
    relay_send_sem,
    relay_recv_sem,
):
    stations, antennas, _, users, tones = guess.shape
    pieces = stations * antennas
    block = PEER_MAX * CU
    clusters = serving_ref.shape[0]
    me = lax.axis_index("ap")
    part = lax.axis_index("sc")
    node, place = ring_of
    spot = place(me)
    right = node(lax.rem(spot + 1, n))
    left = node(lax.rem(spot + n - 1, n))

    table_copy = pltpu.make_async_copy(table_hbm.at[part], table, table_sem)
    table_copy.start()
    small_copies = []
    for source, into in (
        (cluster_hbm, cluster_ref),
        (serving_hbm, serving_ref),
        (owner_hbm, owner_ref),
        (power_hbm, power_ref),
        (gain_hbm, gain_ref),
        (noise_hbm, noise_ref),
        (received_hbm, received_ref),
    ):
        copy = pltpu.make_async_copy(source, into, small_sem.at[len(small_copies)])
        copy.start()
        small_copies.append(copy)
    guess_copies = []
    for q in range(pieces):
        a, i = q // antennas, q % antennas
        copy = pltpu.make_async_copy(guess_hbm.at[a, i], guess.at[a, i], guess_sem.at[q])
        copy.start()
        guess_copies.append(copy)

    barrier = pltpu.get_barrier_semaphore()
    pl.semaphore_signal(barrier, inc=1, device_id={"sc": 1 - part}, device_id_type=MESH)
    for k in range(1, n):
        pl.semaphore_signal(
            barrier, inc=1, device_id={"ap": lax.rem(me + k, n)}, device_id_type=MESH
        )

    for copy in small_copies:
        copy.wait()
    owner_u, rank_u, served_u, before_u, serve_u, position = user_tables(
        cluster_ref[...], serving_ref[...], owner_ref[...], clusters, users, stations, n
    )
    mef = me.astype(jnp.float32)
    mine = iota((n, users), 0) == mef
    served_me = jnp.sum(jnp.where(mine, served_u, 0.0), axis=0, keepdims=True)
    before_me = jnp.sum(jnp.where(mine, before_u, 0.0), axis=0, keepdims=True)
    target = jnp.where(
        served_me > 0.5, owner_u * block + before_me * CU + position, -1.0
    )
    pick[...] = jnp.where(iota((n * block, users), 0) == target, 1.0, 0.0).astype(jnp.bfloat16)
    wide = jnp.broadcast_to(power_ref[...] * (1.0 / users), (LANES, users))
    power_wide[...] = jnp.transpose(wide)

    pl.semaphore_wait(barrier, n)

    gain_copies = []
    for k in range(1, n):
        peer = lax.rem(me + k, n)
        copy = pltpu.make_async_remote_copy(
            src_ref=gain_ref,
            dst_ref=gains.at[me],
            send_sem=gain_send_sem.at[k],
            recv_sem=gain_recv_sem.at[n - k],
            device_id={"ap": peer},
            device_id_type=MESH,
        )
        copy.start()
        gain_copies.append(copy)
    gains[me] = gain_ref[...]

    table_copy.wait()
    half_copies = []
    contract = (((1,), (1,)), ((), ()))
    for q in range(pieces):
        a, i = q // antennas, q % antennas
        guess_copies[q].wait()
        sums = lax.dot_general(
            guess[a, i, 0], table[:, :tones], contract, preferred_element_type=jnp.float32
        ) + lax.dot_general(
            guess[a, i, 1], table[:, tones:], contract, preferred_element_type=jnp.float32
        )
        half[q] = (sums * (1.0 / TONE_NUMBER)).astype(jnp.bfloat16)
        copy = pltpu.make_async_remote_copy(
            src_ref=half.at[q],
            dst_ref=other.at[q],
            send_sem=half_send_sem.at[q],
            recv_sem=half_recv_sem.at[q],
            device_id={"sc": 1 - part},
            device_id_type=MESH,
        )
        copy.start()
        half_copies.append(copy)
    for q in range(pieces):
        half_copies[q].wait_recv()
        total = (half[q].astype(jnp.float32) + other[q].astype(jnp.float32)).astype(jnp.bfloat16)
        coef_b[pl.ds(q * users, users), :] = total
        chosen = jnp.dot(pick[...], total, preferred_element_type=jnp.float32)
        coef_send[:, q] = chosen.astype(jnp.bfloat16).reshape(n, block, 2 * TAPS)
    coef_copies = []
    mine_half = pl.ds(part * (pieces // 2), pieces // 2)
    for k in range(1, n):
        peer = lax.rem(me + k, n)
        copy = pltpu.make_async_remote_copy(
            src_ref=coef_send.at[peer, mine_half],
            dst_ref=coef_all.at[me, mine_half],
            send_sem=coef_send_sem.at[k],
            recv_sem=coef_recv_sem.at[n - k],
            device_id={"ap": peer},
            device_id_type=MESH,
        )
        copy.start()
        coef_copies.append(copy)
    own_coef = pltpu.make_async_copy(coef_send.at[me], coef_all.at[me], local_sem)
    own_coef.start()

    width = tones // chunks
    symbols = received_ref.shape[3]
    rows = stations * symbols
    ring_copies = {}
    reach = {}
    for c in range(chunks):
        far, near = n // 2, n - 1 - n // 2
        reach[c] = (far, near) if c % 2 == 0 else (near, far)

    ready = []

    def origin_of(direction, step):
        back = lax.rem(spot + n - step, n) if direction == 0 else lax.rem(spot + step, n)
        return node(back)

    def ring_start(c, direction, step):
        if step > reach[c][direction]:
            return
        origin = origin_of(direction, step)
        source = own.at[c]
        if step > 0:
            ring_copies[c, direction, step - 1].wait_recv()
            source = solved_all.at[origin, c]
            ready.append((origin, c, source))
        if step == reach[c][direction]:
            return
        copy = pltpu.make_async_remote_copy(
            src_ref=source,
            dst_ref=solved_all.at[origin, c],
            send_sem=ring_send_sem.at[direction, c, step],
            recv_sem=ring_recv_sem.at[direction, c, step],
            device_id={"ap": right if direction == 0 else left},
            device_id_type=MESH,
        )
        copy.start()
        ring_copies[c, direction, step] = copy

    steps = max(max(r) for r in reach.values())
    entries = [(i, j) for i in range(antennas) for j in range(i + 1)]
    noise = jnp.concatenate(
        [
            jnp.broadcast_to(noise_ref[0:1, a : a + 1], (symbols, 1))
            for a in range(stations)
        ],
        axis=0,
    )
    for c in range(chunks):
        base = c * width
        for reim in range(2):
            columns = table[:, reim * tones + base : reim * tones + base + width]
            smooth[reim] = jnp.dot(coef_b[...], columns, preferred_element_type=jnp.float32)
        for a in range(stations):
            for l in range(width // LANES):
                lanes = pl.ds(l * LANES, LANES)

                def body(step, sums, a=a, lanes=lanes):
                    sums = list(sums)
                    for w in range(2):
                        row = (step * 2 + w) * 8
                        scale = power_wide[pl.ds(pl.multiple_of(row, 8), 8), :]
                        re, im = [], []
                        for i in range(antennas):
                            at = pl.multiple_of((a * antennas + i) * users + row, 8)
                            re.append(smooth[0, pl.ds(at, 8), lanes])
                            im.append(smooth[1, pl.ds(at, 8), lanes])
                        at = 0
                        for i in range(antennas):
                            sre, sim = re[i] * scale, im[i] * scale
                            for j in range(i + 1):
                                sums[at] = sums[at] + (sre * re[j] + sim * im[j])
                                at += 1
                                if j < i:
                                    sums[at] = sums[at] + (sim * re[j] - sre * im[j])
                                    at += 1
                    return tuple(sums)

                zero = jnp.zeros((8, LANES), jnp.float32)
                sums = lax.fori_loop(0, users // 16, body, (zero,) * (antennas * antennas))
                for e in range(antennas * antennas):
                    value = jnp.sum(sums[e], axis=0, keepdims=True)
                    cov[e, a * symbols : (a + 1) * symbols, lanes] = jnp.broadcast_to(
                        value, (symbols, LANES)
                    )
        cov_re = [[None] * antennas for _ in range(antennas)]
        cov_im = [[None] * antennas for _ in range(antennas)]
        at = 0
        for i, j in entries:
            cov_re[i][j] = cov[at]
            at += 1
            if i == j:
                cov_re[i][j] = cov_re[i][j] + noise
            else:
                cov_im[i][j] = cov[at]
                at += 1
        signal = []
        for i in range(antennas):
            signal.append(
                tuple(
                    jnp.concatenate(
                        [
                            received_ref[a, i, reim, :, base : base + width].astype(jnp.float32)
                            for a in range(stations)
                        ],
                        axis=0,
                    )
                    for reim in range(2)
                )
            )
        solved = hermitian_solve(cov_re, cov_im, signal)
        for i in range(antennas):
            joined = jnp.concatenate([solved[i][0], solved[i][1]], axis=0)
            own[c, pl.ds(i * 2 * rows, 2 * rows), :] = joined.astype(jnp.bfloat16)
        ready.append((me, c, own.at[c]))
        for d in range(c + 1):
            for direction in range(2):
                ring_start(d, direction, c - d)

    for copy in gain_copies:
        copy.wait_recv()
    weights = []
    totals = jnp.zeros((1, users), jnp.float32)
    for p in range(n):
        for a in range(stations):
            row = serve_u[p * stations + a : p * stations + a + 1] * gains[p, a : a + 1, :]
            weights.append(row)
            totals = totals + row
    scale = 1.0 / (1.0 + totals)
    for p in range(n):
        goal = jnp.where(
            (owner_u == mef) & (served_u[p : p + 1] > 0.5),
            before_u[p : p + 1] * CU + position,
            -1.0,
        )
        hits = iota((block, users), 0) == goal
        for a in range(stations):
            value = jnp.sum(
                jnp.where(hits, weights[p * stations + a] * scale, 0.0), axis=1, keepdims=True
            )
            wrow_ref[p, a] = jnp.broadcast_to(value, (block, LANES))
        for k in range(PEER_MAX):
            value = jnp.sum(
                jnp.where(hits[k * CU : k * CU + 1], rank_u, 0.0), axis=1, keepdims=True
            )
            rank_ref[p * PEER_MAX + k : p * PEER_MAX + k + 1, :] = jnp.broadcast_to(
                value, (1, LANES)
            ).astype(jnp.int32)


    relay_copies = []
    for k in range(1, n):
        coef_copies[n - k - 1].wait_recv()
        origin = lax.rem(me + n - (n - k), n)
        copy = pltpu.make_async_remote_copy(
            src_ref=coef_all.at[origin, mine_half],
            dst_ref=coef_all.at[origin, mine_half],
            send_sem=relay_send_sem.at[k],
            recv_sem=relay_recv_sem.at[k],
            device_id={"sc": 1 - part},
            device_id_type=MESH,
        )
        copy.start()
        relay_copies.append(copy)
    own_coef.wait()

    def combine(origin, c, source):
        base = c * width
        solved_wide[...] = source[...].astype(jnp.float32)
        coefs = coef_all[origin].reshape(pieces * block, 2 * TAPS)
        for reim in range(2):
            columns = table[:, reim * tones + base : reim * tones + base + width]
            smooth[reim, : pieces * block, :] = jnp.dot(
                coefs, columns, preferred_element_type=jnp.float32
            )

        def tile(l, carry):
            lanes = pl.ds(pl.multiple_of(l * LANES, LANES), LANES)
            sums = [[[None, None] for _ in range(symbols)] for _ in range(PEER_MAX)]
            for a in range(stations):
                weight = [wrow_ref[origin, a, pl.ds(k * CU, CU), :] for k in range(PEER_MAX)]
                for i in range(antennas):
                    re, im = [], []
                    for k in range(PEER_MAX):
                        at = (a * antennas + i) * block + k * CU
                        re.append(smooth[0, pl.ds(at, CU), lanes] * weight[k])
                        im.append(smooth[1, pl.ds(at, CU), lanes] * weight[k])
                    for s in range(symbols):
                        first = i * 2 * rows + a * symbols + s
                        sre = solved_wide[pl.ds(first, 1), lanes]
                        sim = solved_wide[pl.ds(first + rows, 1), lanes]
                        for k in range(PEER_MAX):
                            new_re = re[k] * sre + im[k] * sim
                            new_im = re[k] * sim - im[k] * sre
                            old = sums[k][s]
                            if old[0] is not None:
                                new_re, new_im = old[0] + new_re, old[1] + new_im
                            sums[k][s] = [new_re, new_im]
            for k in range(PEER_MAX):
                for s in range(symbols):
                    for reim in range(2):
                        share_ref[
                            c * (width // LANES) + l,
                            origin * PEER_MAX + k,
                            pl.ds((s * 2 + reim) * CU, CU),
                            :,
                        ] = sums[k][s][reim]
            return carry

        lax.fori_loop(0, width // LANES, tile, 0)

    def drain(most):
        for _ in range(most):
            if ready:
                combine(*ready.pop(0))

    late_slots = range(chunks, chunks + steps)
    for late in late_slots:
        for d in range(chunks):
            for direction in range(2):
                if late - d > 0:
                    ring_start(d, direction, late - d)
        if late == chunks:
            for copy in relay_copies:
                copy.wait_recv()
        drain(-(-n * chunks // (steps + 1)))
    drain(len(ready))
    for copy in relay_copies:
        copy.wait_send()
    for copy in half_copies:
        copy.wait_send()
    for copy in gain_copies:
        copy.wait_send()
    for copy in coef_copies:
        copy.wait_send()
    for copy in ring_copies.values():
        copy.wait_send()


def second_kernel(n, rank_ref, share_ref, out_hbm, total, moved, out_sem):
    tiles, _, rows, _ = share_ref.shape
    pairs = rows // (2 * CU)
    height = CU * pairs * tiles * 2
    total[...] = jnp.zeros_like(total)
    slots = [rank_ref[k, 0] for k in range(n * PEER_MAX)]

    def tile(l, carry):
        for k in range(n * PEER_MAX):
            total[l, slots[k]] += share_ref[l, k]
        return carry

    lax.fori_loop(0, tiles, tile, 0)
    copies = []
    for r in range(OWN_MAX):

        def move(l, carry, r=r):
            for s in range(pairs):
                for reim in range(2):
                    moved[pl.ds(r * height + (s * tiles + l) * 2 + reim, CU, stride=pairs * tiles * 2), :] = (
                        total[l, r, pl.ds((s * 2 + reim) * CU, CU), :]
                    )
            return carry

        lax.fori_loop(0, tiles, move, 0)
        part = pl.ds(r * height, height)
        copy = pltpu.make_async_copy(moved.at[part], out_hbm.at[part], out_sem.at[r])
        copy.start()
        copies.append(copy)
    for copy in copies:
        copy.wait()


def ring_functions(mesh):
    n = mesh.shape["ap"]
    half = n // 2

    def plain(q):
        return q

    def node(q):
        upper = q // half
        return (1 - upper) * 2 * q + upper * (2 * (n - q) - 1)

    def place(d):
        odd = d % 2
        return (1 - odd) * (d // 2) + odd * (n - (d + 1) // 2)

    if n % 2:
        return plain, plain
    try:
        axes = list(mesh.axis_names)
        line = np.moveaxis(mesh.devices, axes.index("ap"), 0).reshape(n, -1)[:, 0]
        spots = [tuple(d.coords) for d in line]
        sizes = [max(s[x] for s in spots) + 1 for x in range(3)]

        def length(order):
            far = 0
            for q in range(n):
                one, two = spots[order(q)], spots[order((q + 1) % n)]
                far += sum(
                    min(abs(one[x] - two[x]), sizes[x] - abs(one[x] - two[x])) for x in range(3)
                )
            return far

        if length(plain) < length(node):
            return plain, plain
    except (AttributeError, TypeError):
        pass
    return node, place


def local(
    n,
    parts,
    ring_of,
    unsmoothed_link_guesses,
    received,
    user_power,
    noise_power,
    ap_gain,
    user_cluster,
    serving,
    cluster_owner,
):
    stations, antennas, _, users, tones = unsmoothed_link_guesses.shape
    symbols = received.shape[3]
    pieces = stations * antennas
    block = PEER_MAX * CU
    rows = stations * symbols
    chunks = 2
    width = tones // chunks
    steps = n // 2
    table = jnp.asarray(delay_tables(parts, tones))
    vmem = pl.BlockSpec(memory_space=pltpu.VMEM)
    smem = pl.BlockSpec(memory_space=pltpu.SMEM)
    anywhere = pl.BlockSpec(memory_space=pl.ANY)
    dma = pltpu.SemaphoreType.DMA
    bf16, f32 = jnp.bfloat16, jnp.float32
    hbm = pl.BlockSpec(memory_space=pltpu.HBM)
    tiles = tones // LANES
    held = 4 * LANES * n * PEER_MAX * (tiles * symbols * 2 * CU + 1)
    share, rank = pl.pallas_call(
        functools.partial(first_kernel, n, chunks, ring_of),
        out_shape=(
            jax.ShapeDtypeStruct((tiles, n * PEER_MAX, symbols * 2 * CU, LANES), f32),
            jax.ShapeDtypeStruct((n * PEER_MAX, LANES), jnp.int32),
        ),
        in_specs=[hbm] * 9,
        out_specs=(vmem, vmem),
        scratch_shapes=[
            pltpu.VMEM((n, pieces, block, 2 * TAPS), bf16),
            pltpu.VMEM((n, chunks, antennas * 2 * rows, width), bf16),
            pltpu.VMEM((n, stations, block, LANES), f32),
            pltpu.VMEM(received.shape, bf16),
            pltpu.VMEM((1, users), f32),
            pltpu.VMEM((1, stations), f32),
            pltpu.VMEM((stations, users), f32),
            pltpu.VMEM((1, users), jnp.int32),
            pltpu.VMEM(serving.shape, jnp.int32),
            pltpu.VMEM((1, serving.shape[0]), jnp.int32),
            pltpu.VMEM((antennas * 2 * rows, width), f32),
            pltpu.VMEM((stations, antennas, 2, users, tones), bf16),
            pltpu.VMEM((2 * TAPS, 2 * tones), bf16),
            pltpu.VMEM((pieces, users, 2 * TAPS), bf16),
            pltpu.VMEM((pieces, users, 2 * TAPS), bf16),
            pltpu.VMEM((n, pieces, block, 2 * TAPS), bf16),
            pltpu.VMEM((pieces * users, 2 * TAPS), bf16),
            pltpu.VMEM((n, stations, users), f32),
            pltpu.VMEM((n * block, users), bf16),
            pltpu.VMEM((users, LANES), f32),
            pltpu.VMEM((2, pieces * users, width), f32),
            pltpu.VMEM((antennas * antennas, rows, width), f32),
            pltpu.VMEM((chunks, antennas * 2 * rows, width), bf16),
            dma((pieces,)),
            dma,
            dma((pieces,)),
            dma((pieces,)),
            dma((n,)),
            dma((n,)),
            dma((n,)),
            dma((n,)),
            dma((2, chunks, steps)),
            dma((2, chunks, steps)),
            dma,
            dma((7,)),
            dma((n,)),
            dma((n,)),
        ],
        compiler_params=pltpu.CompilerParams(
            collective_id=0, has_side_effects=True, vmem_limit_bytes=VMEM_BYTES - held
        ),
        name="smooth_solve_combine",
    )(
        unsmoothed_link_guesses,
        received,
        user_power.reshape(1, users),
        noise_power.reshape(1, stations),
        ap_gain,
        user_cluster.reshape(1, users),
        serving,
        cluster_owner.reshape(1, -1),
        table,
    )
    lines = OWN_MAX * CU * symbols * tiles * 2
    placed = pl.pallas_call(
        functools.partial(second_kernel, n),
        out_shape=jax.ShapeDtypeStruct((lines, LANES), f32),
        in_specs=[smem, vmem],
        out_specs=hbm,
        scratch_shapes=[
            pltpu.VMEM((tiles, OWN_MAX, symbols * 2 * CU, LANES), f32),
            pltpu.VMEM((lines, LANES), f32),
            dma((OWN_MAX,)),
        ],
        compiler_params=pltpu.CompilerParams(vmem_limit_bytes=16 * 1024 * 1024),
        name="place",
    )(rank, share)
    placed = placed.reshape(OWN_MAX, CU, symbols, tiles, 2, LANES)
    placed = jnp.transpose(placed, (0, 1, 2, 4, 3, 5))
    return placed.reshape(OWN_MAX, CU, symbols, 2, tones)


def solution(mesh):
    placed = (
        P(("cell", "ap"), None, None, None, "sc"),
        P(("cell", "ap"), None, None, None, "sc"),
        P("cell"),
        P(("cell", "ap")),
        P(("cell", "ap"), None),
        P("cell"),
        P("cell", None),
        P("cell", None),
    )
    return jax.shard_map(
        functools.partial(local, mesh.shape["ap"], mesh.shape["sc"], ring_functions(mesh)),
        mesh=mesh,
        in_specs=placed,
        out_specs=P(("cell", "ap"), None, None, None, "sc"),
        check_vma=False,
    )
```
